32 devices in a mesh: gx: 2 (over y), gy: 4 (over z), gz: 4 (over x, core).
Axes of the slice: x: 2, y: 2, z: 4, core: 2. Of those that a mesh axis runs over, the one named last changes fastest.
Arguments:
- features: bfloat16 [64, 2, 4, 8192], P(None, 'gx', 'gy', 'gz'), may hold values from -6 to 6
- tiles: bfloat16 [2, 4, 128, 64, 512], P('gx', 'gy', 'gz'), may hold values from -0.25 to 0.25
- scales: float32 [2, 4, 128, 8], P('gx', 'gy', 'gz'), may hold values from 0.5 to 2
- slots: int32 [2, 4, 128, 8], P('gx', 'gy', 'gz'), may hold values from 0 to 175, as said below
- live: int32 [2, 4, 128], P('gx', 'gy', 'gz'), may hold values from 2 to 8, as said below
- times: float32 [64], replicated, may hold values from 0.6 to 1.6
Outputs:
- diffused: bfloat16 [64, 2, 4, 8192], P(None, 'gx', 'gy', 'gz')
The draws below stay inside these ranges and needn't reach their ends.
Inputs may be any that keep to these rules, and one draw needn't show every extreme that they name: Slot 0 of every block row is the row's own block; slots 1 to 3 hold blocks of the row's own device, the others blocks from the shared set. `live`: each device has some block row with all 8 slots used.
All inputs are finite; a program needn't handle non-finite values.
Results may differ from the reference program's by a relative error of at most 0.0032.
Values may be sent and summed in bfloat16 or wider, within the bound.
No kernel may reach another device: no remote copies, remote signals or barrier semaphores. Data moves between devices by JAX's collectives and lax.ppermute only.
A program may use at most 64 MiB of HBM per device.

```python
import math
import jax
import jax.numpy as jnp
from jax import lax

F = 64
PB = 64
K = 8
TERMS = 3
BLK = 32
RIM = 4
GXT = 2
GYT = 4
NZB = 128
ZP = 8192
SHARED = 144
N_GZ = 4


def draw_slots(key, part):
    shape = (GXT, GYT, NZB, K)
    key_near, key_far = jax.random.split(jax.random.fold_in(key, 11))
    own = lax.broadcasted_iota(jnp.int32, shape, 2) % BLK
    near = jax.random.randint(key_near, shape, 0, BLK)
    far = jax.random.randint(key_far, shape, BLK, BLK + SHARED)
    column = lax.broadcasted_iota(jnp.int32, shape, 3)
    return jnp.where(column == 0, own, jnp.where(column < K // 2, near, far)).astype(jnp.int32)


def draw_live(key, part):
    shape = (GXT, GYT, NZB)
    counts = jax.random.randint(jax.random.fold_in(key, 23), shape, 2, K + 1)
    first = lax.broadcasted_iota(jnp.int32, shape, 2) % BLK == 0
    return jnp.where(first, K, counts).astype(jnp.int32)


def levels(own_key, dims, pieces, smallest, largest):
    def one(axis_at, shards_of):
        heights = jax.random.uniform(jax.random.fold_in(jax.random.fold_in(own_key, 6), axis_at), (shards_of,), jnp.float32, smallest / len(pieces), largest / len(pieces))
        return jnp.repeat(jnp.exp(heights), dims[axis_at] // shards_of).reshape((-1,) + (1,) * (len(dims) - axis_at - 1))

    gain = one(*pieces[0])
    for cut in pieces[1:]:
        gain = gain * one(*cut)
    return gain


def gaussian(stream_key, shape, deviation, limit, cuts=(), held_as=jnp.bfloat16):
    array = deviation * jax.random.normal(stream_key, shape, jnp.float32)
    if cuts:
        array = array * levels(stream_key, shape, cuts, -0.22, 0.18)
    return jnp.clip(array, -limit, limit).astype(held_as)


def setup_inputs(seed: int = 0) -> dict:
    keys = jax.random.split(jax.random.key(seed), 7)
    return {
        "features": gaussian(keys[0], (F, GXT, GYT, ZP), 1.0, 6.0, ((1, 2), (2, 4), (3, 4))),
        "tiles": gaussian(keys[1], (GXT, GYT, NZB, PB, K * PB), (K * PB) ** -0.5, 0.25, ((0, 2), (1, 4), (2, 4))),
        "scales": jnp.clip(jnp.exp(math.log(2.0) - 1.3862944 * jax.random.uniform(keys[2], (GXT, GYT, NZB, K), jnp.float32) ** levels(keys[2], (GXT, GYT, NZB, K), ((0, 2), (1, 4), (2, 4)), -0.2, 0.2)), 0.5, 2.0),
        "slots": draw_slots(jax.random.fold_in(keys[6], 71), 0),
        "live": draw_live(jax.random.fold_in(keys[6], 71), 0),
        "times": jnp.clip(jnp.exp(jax.random.uniform(keys[5], (F,), jnp.float32, math.log(0.6), math.log(1.6))), 0.6, 1.6),
    }


def apply_operator(value, tiles, scales, slots, live):
    width_x = value.shape[1]
    width_y = value.shape[2]
    layers = N_GZ
    ndev = width_x * width_y * layers
    blocks = value.reshape(F, width_x, width_y, layers, BLK, PB).transpose(1, 2, 3, 4, 0, 5)
    blocks = blocks.reshape(width_x, width_y, layers, BLK, F * PB)
    padded = jnp.pad(blocks, ((1, 1), (1, 1), (0, 0), (0, 0), (0, 0)))
    flat = padded.reshape(-1, F * PB)
    dev_ids = jnp.arange(ndev, dtype=jnp.int32)
    tile_dev = tiles.reshape(ndev, BLK, PB, K * PB)
    slot_dev = slots.reshape(ndev, BLK, K)
    scale_dev = scales.reshape(ndev, BLK, K)
    live_dev = live.reshape(ndev, BLK)

    def one_device(items):
        dev, tile, slot, scale, count = items
        row_i = dev // (width_y * layers)
        row_j = (dev // layers) % width_y
        row_l = dev % layers
        local = slot < BLK
        rest = jnp.maximum(slot - BLK, 0)
        rim_pos = rest % RIM
        layer_pos = (rest // RIM) % layers
        col_y = (rest // (RIM * layers)) % 3
        col_x = rest // (RIM * layers * 3)
        grid_i = jnp.where(local, row_i + 1, row_i + col_x)
        grid_j = jnp.where(local, row_j + 1, row_j + col_y)
        grid_l = jnp.where(local, row_l, layer_pos)
        grid_b = jnp.where(local, slot, rim_pos)
        index = (((grid_i * (width_y + 2) + grid_j) * layers + grid_l) * BLK + grid_b).astype(jnp.int32)
        picked = flat[index.reshape(-1)].reshape(BLK, K, F, PB)
        product = jnp.einsum('bkfc,brkc->bkfr', picked.astype(jnp.float32),
                             tile.reshape(BLK, PB, K, PB).astype(jnp.float32))
        used = (lax.broadcasted_iota(jnp.int32, (BLK, K), 1) < count[:, None]).astype(jnp.float32)
        return jnp.einsum('bkfr,bk->bfr', product, scale * used)

    result = lax.map(one_device, (dev_ids, tile_dev, slot_dev, scale_dev, live_dev))
    result = result.reshape(width_x, width_y, layers, BLK, F, PB).transpose(4, 0, 1, 2, 3, 5)
    return result.reshape(F, width_x, width_y, layers * BLK * PB)


def reference(features, tiles, scales, slots, live, times):
    total = features.astype(jnp.float32)
    factor = jnp.ones((F,), jnp.float32)
    value = features
    for term in range(1, TERMS + 1):
        image = apply_operator(value, tiles, scales, slots, live)
        factor = factor * (-times) / jnp.float32(term)
        total = total + factor[:, None, None, None] * image
        value = image.astype(jnp.bfloat16)
    return total.astype(jnp.bfloat16)
```

```python
import functools

import jax
import jax.numpy as jnp
from jax import lax
from jax.experimental import pallas as pl
from jax.experimental.pallas import tpu as pltpu
from jax.sharding import PartitionSpec as P

PB = 64
TERMS = 3
LANES = 2 * PB


def pairings(count):
    first = [(i, i ^ 1) for i in range(count)]
    second = [(i, (i + 1) % count if i % 2 else (i - 1) % count) for i in range(count)]
    return [first] if count == 2 else [first, second]


def partner_rank(here, step, count):
    forward = jnp.where(here % 2 == 0, 1, 2)
    backward = 3 - forward
    rank = jnp.where(step == 1, 0, jnp.where(step == 2, forward, backward))
    there = here + step - 1
    return rank, (there >= 0) & (there < count)


def exchange(rim):
    rows = jnp.stack([rim] + [lax.ppermute(rim, "gy", p) for p in pairings(lax.axis_size("gy"))])
    if lax.axis_size("gx") == 2:
        both = lax.all_gather(rows, ("gx", "gz"), axis=0, tiled=False)
        return both
    grid = jnp.stack([rows] + [lax.ppermute(rows, "gx", p) for p in pairings(lax.axis_size("gx"))])
    return lax.all_gather(grid, "gz", axis=0, tiled=False)


def source_index(slots, count, rim_count):
    layers = lax.axis_size("gz")
    x_size, y_size = lax.axis_size("gx"), lax.axis_size("gy")
    x_at, y_at = lax.axis_index("gx"), lax.axis_index("gy")
    rest = jnp.maximum(slots - count, 0)
    r = rest % rim_count
    m = (rest // rim_count) % layers
    c = (rest // (rim_count * layers)) % 3
    a = rest // (rim_count * layers * 3)
    y_rank, y_in = partner_rank(y_at, c, y_size)
    y_count = len(pairings(y_size)) + 1
    if x_size == 2:
        x_there = x_at + a - 1
        x_in = (x_there >= 0) & (x_there < 2)
        panel = (x_there * layers + m) * y_count + y_rank
        panels = 2 * layers * y_count
    else:
        x_rank, x_in = partner_rank(x_at, a, x_size)
        x_count = len(pairings(x_size)) + 1
        panel = (m * x_count + x_rank) * y_count + y_rank
        panels = layers * x_count * y_count
    far = count + panel * rim_count + r
    zero = count + panels * rim_count
    index = jnp.where(slots < count, slots, jnp.where(x_in & y_in, far, zero))
    return index.astype(jnp.int32), panels


def term_kernel(index_ref, value_ref, far_ref, tile_ref, total_ref, factor_ref, *rest, last):
    if last:
        total_out, source = rest
    else:
        value_out, rim_out, total_out, source = rest
    features, points = value_ref.shape
    panels, _, rim = far_ref.shape
    count = points // PB
    slot_count = tile_ref.shape[1] // PB
    left = lax.broadcasted_iota(jnp.int32, (features, LANES), 1) < PB

    def spread(pair, at):
        turned = jnp.concatenate([pair[:, PB:], pair[:, :PB]], axis=1)
        source[at] = jnp.where(left, pair, turned)
        source[at + 1] = jnp.where(left, turned, pair)

    for t in range(points // LANES):
        spread(value_ref[:, t * LANES : (t + 1) * LANES], 2 * t)

    @pl.loop(0, panels)
    def _(panel):
        for t in range(rim // LANES):
            spread(
                far_ref[panel, :, t * LANES : (t + 1) * LANES],
                count + panel * (rim // PB) + 2 * t,
            )

    source[count + panels * (rim // PB)] = jnp.zeros((features, LANES), source.dtype)
    factor = factor_ref[...]

    def picked(row):
        base = row * slot_count
        return jnp.concatenate(
            [
                jnp.where(left, source[index_ref[base + k]], source[index_ref[base + k + 1]])
                for k in range(0, slot_count, 2)
            ],
            axis=1,
        )

    for t in range(points // LANES):
        at = pl.ds(t * LANES, LANES)
        both = lax.dot_general(
            jnp.concatenate([picked(2 * t), picked(2 * t + 1)], axis=0),
            tile_ref[at, :],
            (((1,), (1,)), ((), ())),
            preferred_element_type=jnp.float32,
        )
        image = jnp.where(left, both[:features], both[features:])
        total = total_ref[:, at].astype(jnp.float32) + factor * image
        total_out[:, at] = total.astype(total_out.dtype)
        if not last:
            rounded = image.astype(value_out.dtype)
            value_out[:, at] = rounded
            if t < rim // LANES:
                rim_out[:, at] = rounded


def term(index, value, far, tiles, total, factor, last):
    features, points = value.shape
    vmem = pl.BlockSpec(memory_space=pltpu.VMEM)
    whole = jax.ShapeDtypeStruct(value.shape, jnp.bfloat16)
    if last:
        out_shape = whole
        out_specs = vmem
    else:
        out_shape = (
            whole,
            jax.ShapeDtypeStruct((features, far.shape[2]), jnp.bfloat16),
            jax.ShapeDtypeStruct(value.shape, jnp.float32),
        )
        out_specs = (vmem,) * 3
    blocks = points // PB + far.shape[0] * (far.shape[2] // PB) + 1
    return pl.pallas_call(
        functools.partial(term_kernel, last=last),
        out_shape=out_shape,
        in_specs=[pl.BlockSpec(memory_space=pltpu.SMEM)] + [vmem] * 5,
        out_specs=out_specs,
        scratch_shapes=[pltpu.VMEM((blocks, features, LANES), jnp.bfloat16)],
        compiler_params=pltpu.CompilerParams(vmem_limit_bytes=32 * 1024 * 1024),
        cost_estimate=pl.CostEstimate(
            flops=2 * features * tiles.size, bytes_accessed=2 * tiles.size, transcendentals=0
        ),
    )(index, value, far, tiles, total, factor)


def body(features, tiles, scales, slots, live, times):
    count, width = tiles.shape[2], tiles.shape[4]
    slot_count = scales.shape[3]
    size = features.shape[0]
    rim_count = max(1, count // 8)
    value = features.reshape(size, count * PB)
    rim = value[:, : rim_count * PB]
    index, panels = source_index(slots.reshape(count * slot_count), count, rim_count)
    used = lax.broadcasted_iota(jnp.int32, (count, slot_count), 1) < live.reshape(count, 1)
    weights = scales.reshape(count, slot_count) * used.astype(jnp.float32)
    lanes = jnp.repeat(weights, PB, axis=1)
    scaled = tiles.reshape(count, PB, width).astype(jnp.float32) * lanes[:, None, :]
    scaled = scaled.astype(jnp.bfloat16).reshape(count * PB, width)
    total = value
    factor = jnp.ones(times.shape, jnp.float32)
    for step in range(1, TERMS + 1):
        far = exchange(rim).reshape(panels, size, rim_count * PB)
        factor = factor * -times / jnp.float32(step)
        out = term(index, value, far, scaled, total, factor[:, None], step == TERMS)
        if step < TERMS:
            value, rim, total = out
    return out.reshape(features.shape)


def solution(mesh):
    return jax.shard_map(
        body,
        mesh=mesh,
        in_specs=(
            P(None, "gx", "gy", "gz"),
            P("gx", "gy", "gz", None, None),
            P("gx", "gy", "gz", None),
            P("gx", "gy", "gz", None),
            P("gx", "gy", "gz"),
            P(),
        ),
        out_specs=P(None, "gx", "gy", "gz"),
        check_vma=False,
    )
```

```python
import functools

import jax
import jax.numpy as jnp
from jax import lax
from jax.experimental import pallas as pl
from jax.experimental.pallas import tpu as pltpu
from jax.sharding import PartitionSpec as P

PB = 64
TERMS = 3
LANES = 2 * PB
AXES = ("gx", "gy", "gz")


def pairings(count):
    first = [(i, i ^ 1) for i in range(count)]
    second = [(i, (i + 1) % count if i % 2 else (i - 1) % count) for i in range(count)]
    return [first] if count == 2 else [first, second]


def partner_rank(here, step, count):
    forward = jnp.where(here % 2 == 0, 1, 2)
    backward = 3 - forward
    rank = jnp.where(step == 1, 0, jnp.where(step == 2, forward, backward))
    there = here + step - 1
    return rank, (there >= 0) & (there < count)


def place(rank, here, count):
    return here if rank == 0 else dict(pairings(count)[rank - 1])[here]


def partners():
    x_count = len(pairings(lax.axis_size("gx"))) + 1
    y_count = len(pairings(lax.axis_size("gy"))) + 1
    pair_count = lax.axis_size("gz") // 2
    chips = [(x, b) for x in range(x_count) for b in range(pair_count)]
    side = [(x, y, b) for x, b in chips for y in range(1, y_count)]
    return side + [(x, 0, b) for x, b in chips[1:]]


def partner_number(x, y, b):
    x_count = len(pairings(lax.axis_size("gx"))) + 1
    y_count = len(pairings(lax.axis_size("gy"))) + 1
    pair_count = lax.axis_size("gz") // 2
    chip = x * pair_count + b
    return jnp.where(
        y > 0, chip * (y_count - 1) + y - 1, x_count * pair_count * (y_count - 1) + chip - 1
    )


def swap(value, by_core):
    sizes = [lax.axis_size(name) for name in AXES]
    pairs = []
    for i in range(sizes[0]):
        for j in range(sizes[1]):
            for k in range(sizes[2]):
                x, y, b = by_core[k % 2]
                to = (place(x, i, sizes[0]), place(y, j, sizes[1]), (k // 2 ^ b) * 2 + k % 2)
                pairs.append(
                    ((i * sizes[1] + j) * sizes[2] + k, (to[0] * sizes[1] + to[1]) * sizes[2] + to[2])
                )
    return lax.ppermute(value, AXES, pairs)


def swap_cores(value):
    return lax.ppermute(value, "gz", [(k, k ^ 1) for k in range(lax.axis_size("gz"))])


def exchange(rim):
    chips = partners()
    alone = [swap(rim, (chips[-1], chips[-1]))] if len(chips) % 2 else []
    other = swap_cores(rim)
    both = jnp.stack([rim, other])
    shares = [
        swap(both, (chips[t], chips[t + 1])) for t in range(0, len(chips) - len(chips) % 2, 2)
    ]
    received = jnp.concatenate(shares + [panel[None] for panel in alone])
    return received, swap_cores(received), other


def source_index(slots, count, rim_count):
    layers = lax.axis_size("gz")
    x_at, y_at, z_at = (lax.axis_index(name) for name in AXES)
    rest = jnp.maximum(slots - count, 0)
    r = rest % rim_count
    m = (rest // rim_count) % layers
    c = (rest // (rim_count * layers)) % 3
    a = rest // (rim_count * layers * 3)
    x_rank, x_in = partner_rank(x_at, a, lax.axis_size("gx"))
    y_rank, y_in = partner_rank(y_at, c, lax.axis_size("gy"))
    flip = (m // 2) ^ (z_at // 2)
    chips = len(partners())
    core, target = z_at % 2, m % 2
    number = partner_number(x_rank, y_rank, flip)
    single = (number == chips - 1) if chips % 2 else jnp.zeros(number.shape, bool)
    holder = jnp.where(single, target, number % 2)
    panel = jnp.where(single, chips - 1, number // 2 * 2 + (target ^ holder))
    panel = panel + jnp.where(holder == core, 0, chips)
    here = (x_rank == 0) & (y_rank == 0) & (flip == 0)
    panel = jnp.where(here, 2 * chips, panel)
    far = count + panel * rim_count + r
    far = jnp.where(here & (target == core), r, far)
    zero = count + (2 * chips + 1) * rim_count
    index = jnp.where(slots < count, slots, jnp.where(x_in & y_in, far, zero))
    return index.astype(jnp.int32)


def term_kernel(
    index_ref, value_ref, mine_ref, others_ref, other_ref, tile_ref, *rest, kind
):
    if kind == "rim":
        rim_out, source = rest
    elif kind == "full":
        total_ref, factor_ref, value_out, total_out, source = rest
    else:
        total_ref, factor_ref, total_out, source = rest
    features, points = value_ref.shape
    panels, _, rim = mine_ref.shape
    count, rim_count = points // PB, rim // PB
    slot_count = tile_ref.shape[1] // PB
    left = lax.broadcasted_iota(jnp.int32, (features, LANES), 1) < PB

    def spread(pair, at):
        turned = jnp.concatenate([pair[:, PB:], pair[:, :PB]], axis=1)
        source[at] = jnp.where(left, pair, turned)
        source[at + 1] = jnp.where(left, turned, pair)

    for t in range(points // LANES):
        spread(value_ref[:, t * LANES : (t + 1) * LANES], 2 * t)
    for t in range(rim // LANES):
        spread(
            other_ref[:, t * LANES : (t + 1) * LANES], count + 2 * panels * rim_count + 2 * t
        )

    @pl.loop(0, panels)
    def _(panel):
        for t in range(rim // LANES):
            cut = slice(t * LANES, (t + 1) * LANES)
            at = count + panel * rim_count + 2 * t
            spread(mine_ref[panel, :, cut], at)
            spread(others_ref[panel, :, cut], at + panels * rim_count)

    source[count + (2 * panels + 1) * rim_count] = jnp.zeros((features, LANES), source.dtype)

    def picked(row):
        base = row * slot_count
        return jnp.concatenate(
            [
                jnp.where(left, source[index_ref[base + k]], source[index_ref[base + k + 1]])
                for k in range(0, slot_count, 2)
            ],
            axis=1,
        )

    for t in range((rim if kind == "rim" else points) // LANES):
        at = pl.ds(t * LANES, LANES)
        both = lax.dot_general(
            jnp.concatenate([picked(2 * t), picked(2 * t + 1)], axis=0),
            tile_ref[at, :],
            (((1,), (1,)), ((), ())),
            preferred_element_type=jnp.float32,
        )
        image = jnp.where(left, both[:features], both[features:])
        if kind == "rim":
            rim_out[:, at] = image.astype(rim_out.dtype)
            continue
        total = total_ref[:, at].astype(jnp.float32) + factor_ref[...] * image
        total_out[:, at] = total.astype(total_out.dtype)
        if kind == "full":
            value_out[:, at] = image.astype(value_out.dtype)


def term(kind, index, value, rims, tiles, *accumulate):
    features, points = value.shape
    vmem = pl.BlockSpec(memory_space=pltpu.VMEM)
    whole = jax.ShapeDtypeStruct(value.shape, jnp.bfloat16)
    rim = rims[0].shape[2]
    if kind == "rim":
        tiles = tiles[:rim]
        out_shape = jax.ShapeDtypeStruct((features, rim), jnp.bfloat16)
        out_specs = vmem
    elif kind == "full":
        out_shape = (whole, jax.ShapeDtypeStruct(value.shape, jnp.float32))
        out_specs = (vmem, vmem)
    else:
        out_shape, out_specs = whole, vmem
    blocks = points // PB + (2 * rims[0].shape[0] + 1) * (rim // PB) + 1
    return pl.pallas_call(
        functools.partial(term_kernel, kind=kind),
        out_shape=out_shape,
        in_specs=[pl.BlockSpec(memory_space=pltpu.SMEM)] + [vmem] * (5 + len(accumulate)),
        out_specs=out_specs,
        scratch_shapes=[pltpu.VMEM((blocks, features, LANES), jnp.bfloat16)],
        compiler_params=pltpu.CompilerParams(vmem_limit_bytes=32 * 1024 * 1024),
        cost_estimate=pl.CostEstimate(
            flops=2 * features * tiles.size, bytes_accessed=2 * tiles.size, transcendentals=0
        ),
    )(index, value, *rims, tiles, *accumulate)


def body(features, tiles, scales, slots, live, times):
    count, width = tiles.shape[2], tiles.shape[4]
    slot_count = scales.shape[3]
    size = features.shape[0]
    rim_count = max(1, count // 8)
    value = features.reshape(size, count * PB)
    rim = value[:, : rim_count * PB]
    index = source_index(slots.reshape(count * slot_count), count, rim_count)
    used = lax.broadcasted_iota(jnp.int32, (count, slot_count), 1) < live.reshape(count, 1)
    weights = scales.reshape(count, slot_count) * used.astype(jnp.float32)
    lanes = jnp.repeat(weights, PB, axis=1)
    scaled = tiles.reshape(count, PB, width).astype(jnp.float32) * lanes[:, None, :]
    scaled = scaled.astype(jnp.bfloat16).reshape(count * PB, width)
    total = value
    factor = jnp.ones(times.shape, jnp.float32)
    for step in range(1, TERMS + 1):
        rims = exchange(rim)
        factor = factor * -times / jnp.float32(step)
        if step < TERMS:
            rim = term("rim", index, value, rims, scaled)
            value, total = term("full", index, value, rims, scaled, total, factor[:, None])
        else:
            total = term("last", index, value, rims, scaled, total, factor[:, None])
    return total.reshape(features.shape)


def solution(mesh):
    return jax.shard_map(
        body,
        mesh=mesh,
        in_specs=(
            P(None, "gx", "gy", "gz"),
            P("gx", "gy", "gz", None, None),
            P("gx", "gy", "gz", None),
            P("gx", "gy", "gz", None),
            P("gx", "gy", "gz"),
            P(),
        ),
        out_specs=P(None, "gx", "gy", "gz"),
        check_vma=False,
    )
```

```python
import functools

import jax
import jax.numpy as jnp
from jax import lax
from jax.experimental import pallas as pl
from jax.experimental.pallas import tpu as pltpu
from jax.sharding import PartitionSpec as P

PB = 64
TERMS = 3
FEATURES = 64
NEAR = 4
LANES = 2 * PB
AXES = ("gx", "gy", "gz")


def pairings(count):
    first = [(i, i ^ 1) for i in range(count)]
    second = [(i, (i + 1) % count if i % 2 else (i - 1) % count) for i in range(count)]
    return [first] if count == 2 else [first, second]


def partner_rank(here, step, count):
    forward = jnp.where(here % 2 == 0, 1, 2)
    backward = 3 - forward
    rank = jnp.where(step == 1, 0, jnp.where(step == 2, forward, backward))
    there = here + step - 1
    return rank, (there >= 0) & (there < count)


def place(rank, here, count):
    there = here if rank == 0 else dict(pairings(count)[rank - 1])[here]
    return there if abs(there - here) <= 1 else None


def partners():
    x_count = len(pairings(lax.axis_size("gx"))) + 1
    y_count = len(pairings(lax.axis_size("gy"))) + 1
    pair_count = lax.axis_size("gz") // 2
    chips = [(x, b) for x in range(x_count) for b in range(pair_count)]
    side = [(x, y, b) for x, b in chips for y in range(1, y_count)]
    return side + [(x, 0, b) for x, b in chips[1:]]


def partner_number(x, y, b):
    x_count = len(pairings(lax.axis_size("gx"))) + 1
    y_count = len(pairings(lax.axis_size("gy"))) + 1
    pair_count = lax.axis_size("gz") // 2
    chip = x * pair_count + b
    return jnp.where(
        y > 0, chip * (y_count - 1) + y - 1, x_count * pair_count * (y_count - 1) + chip - 1
    )


def swap(value, by_core):
    sizes = [lax.axis_size(name) for name in AXES]
    pairs = []
    for i in range(sizes[0]):
        for j in range(sizes[1]):
            for k in range(sizes[2]):
                x, y, b = by_core[k % 2]
                to = (place(x, i, sizes[0]), place(y, j, sizes[1]), (k // 2 ^ b) * 2 + k % 2)
                if None in to:
                    to = (i, j, (k // 2 ^ 1) * 2 + k % 2)
                pairs.append(
                    ((i * sizes[1] + j) * sizes[2] + k, (to[0] * sizes[1] + to[1]) * sizes[2] + to[2])
                )
    return lax.ppermute(value, AXES, pairs)


def swap_cores(value):
    return lax.ppermute(value, "gz", [(k, k ^ 1) for k in range(lax.axis_size("gz"))])


def exchange(rim, work):
    chips = partners()
    alone = [swap(rim, (chips[-1], chips[-1]))] if len(chips) % 2 else []
    other = swap_cores(rim)
    both = jnp.stack([rim, other])
    steps = reversed(range(0, len(chips) - len(chips) % 2, 2))
    shares = [swap(both, (chips[t], chips[t + 1])) for t in steps][::-1]
    received = jnp.concatenate(shares + [panel[None] for panel in alone])
    received, work = lax.optimization_barrier((received, work))
    return (received, swap_cores(received), other, rim), work


def source_index(slots, count, rim_count):
    layers = lax.axis_size("gz")
    x_at, y_at, z_at = (lax.axis_index(name) for name in AXES)
    rest = jnp.maximum(slots - count, 0)
    r = rest % rim_count
    m = (rest // rim_count) % layers
    c = (rest // (rim_count * layers)) % 3
    a = rest // (rim_count * layers * 3)
    x_rank, x_in = partner_rank(x_at, a, lax.axis_size("gx"))
    y_rank, y_in = partner_rank(y_at, c, lax.axis_size("gy"))
    flip = (m // 2) ^ (z_at // 2)
    chips = len(partners())
    core, target = z_at % 2, m % 2
    number = partner_number(x_rank, y_rank, flip)
    single = (number == chips - 1) if chips % 2 else jnp.zeros(number.shape, bool)
    holder = jnp.where(single, target, number % 2)
    panel = jnp.where(single, chips - 1, number // 2 * 2 + (target ^ holder))
    panel = panel + jnp.where(holder == core, 0, chips)
    here = (x_rank == 0) & (y_rank == 0) & (flip == 0)
    panel = jnp.where(here, 2 * chips + jnp.where(target == core, 1, 0), panel)
    zero = (2 * chips + 2) * rim_count
    far = jnp.where(x_in & y_in, panel * rim_count + r, zero)
    index = jnp.where(slots < count, slots, far)
    return index.astype(jnp.int32)


def left_half():
    return lax.broadcasted_iota(jnp.int32, (FEATURES, LANES), 1) < PB


def turn(pair):
    return jnp.concatenate([pair[:, PB:], pair[:, :PB]], axis=1)


def spread(pair, store, at):
    turned = turn(pair)
    store[at] = jnp.where(left_half(), pair, turned)
    store[at + 1] = jnp.where(left_half(), turned, pair)


def each_rim(rims, place_pair):
    mine_ref, others_ref, other_ref, own_ref = rims
    panels, _, rim = mine_ref.shape
    rim_count = rim // PB

    @pl.loop(0, panels)
    def _(panel):
        for t in range(rim // LANES):
            cut = slice(t * LANES, (t + 1) * LANES)
            at = panel * rim_count + 2 * t
            place_pair(mine_ref[panel, :, cut], at)
            place_pair(others_ref[panel, :, cut], at + panels * rim_count)

    for t in range(rim // LANES):
        cut = slice(t * LANES, (t + 1) * LANES)
        at = 2 * panels * rim_count + 2 * t
        place_pair(other_ref[:, cut], at)
        place_pair(own_ref[:, cut], at + rim_count)


def product(first, second, tile):
    both = lax.dot_general(
        jnp.concatenate([first, second], axis=0),
        tile,
        (((1,), (1,)), ((), ())),
        preferred_element_type=jnp.float32,
    )
    return jnp.where(left_half(), both[:FEATURES], both[FEATURES:])


def picked(store, index_ref, at):
    return jnp.concatenate(
        [
            jnp.where(left_half(), store[index_ref[at + k]], store[index_ref[at + k + 1]])
            for k in range(0, NEAR, 2)
        ],
        axis=1,
    )


def near_image(index_ref, store, tile_ref, near_out):
    slot_count = tile_ref.shape[1] // PB
    for t in range(near_out.shape[1] // LANES):
        at = pl.ds(t * LANES, LANES)
        near_out[:, at] = product(
            picked(store, index_ref, 2 * t * slot_count),
            picked(store, index_ref, (2 * t + 1) * slot_count),
            tile_ref[at, : NEAR * PB],
        )


def first_kernel(index_ref, value_ref, raw_ref, scale_ref, live_ref, tile_out, near_out, store):
    count, slot_count = scale_ref.shape
    used = lax.broadcasted_iota(jnp.int32, (count, slot_count), 1) < live_ref[...]
    weights = jnp.where(used, scale_ref[...], 0.0)
    lanes = jnp.concatenate(
        [jnp.broadcast_to(weights[:, k : k + 1], (count, PB)) for k in range(slot_count)], axis=1
    )
    for b in range(count):
        at = pl.ds(b * PB, PB)
        scaled = raw_ref[at, :].astype(jnp.float32) * lanes[b : b + 1, :]
        tile_out[at, :] = scaled.astype(tile_out.dtype)
    for t in range(value_ref.shape[1] // LANES):
        spread(value_ref[:, t * LANES : (t + 1) * LANES], store, 2 * t)
    near_image(index_ref, store, tile_out, near_out)


def rim_kernel(index_ref, *refs):
    rims, (tile_ref, near_ref, rim_out, store) = refs[:4], refs[4:]
    slot_count = tile_ref.shape[1] // PB

    def keep(pair, number):
        store[number // 2] = pair

    each_rim(rims, keep)
    store[store.shape[0] - 1] = jnp.zeros(store.shape[1:], store.dtype)

    def sources(row):
        base = row * slot_count + NEAR
        parts = []
        for k in range(0, NEAR, 2):
            halves = []
            for side in range(2):
                number = index_ref[base + k + side]
                pair = store[number // 2]
                halves.append(jnp.where(number % 2 == side, pair, turn(pair)))
            parts.append(jnp.where(left_half(), halves[0], halves[1]))
        return jnp.concatenate(parts, axis=1)

    for t in range(rim_out.shape[1] // LANES):
        at = pl.ds(t * LANES, LANES)
        far = product(sources(2 * t), sources(2 * t + 1), tile_ref[at, NEAR * PB :])
        rim_out[:, at] = (near_ref[:, at] + far).astype(rim_out.dtype)


def far_kernel(step, last, index_ref, *refs):
    rims, (tile_ref, near_ref, total_ref, times_ref) = refs[:4], refs[4:8]
    if last:
        total_out, store = refs[8:]
    else:
        total_out, near_out, store, own_store = refs[8:]
    slot_count = tile_ref.shape[1] // PB
    each_rim(rims, lambda pair, number: spread(pair, store, number))
    store[store.shape[0] - 1] = jnp.zeros(store.shape[1:], store.dtype)
    factor = jnp.ones(times_ref.shape, jnp.float32)
    for n in range(1, step + 1):
        factor = factor * -times_ref[...] / jnp.float32(n)
    for t in range(near_ref.shape[1] // LANES):
        at = pl.ds(t * LANES, LANES)
        image = near_ref[:, at] + product(
            picked(store, index_ref, 2 * t * slot_count + NEAR),
            picked(store, index_ref, (2 * t + 1) * slot_count + NEAR),
            tile_ref[at, NEAR * PB :],
        )
        total = total_ref[:, at].astype(jnp.float32) + factor * image
        total_out[:, at] = total.astype(total_out.dtype)
        if not last:
            spread(image.astype(jnp.bfloat16), own_store, 2 * t)
    if not last:
        near_image(index_ref, own_store, tile_ref, near_out)


def call(kernel, out_shape, scratch, flops, index, *arrays):
    vmem = pl.BlockSpec(memory_space=pltpu.VMEM)
    return pl.pallas_call(
        kernel,
        out_shape=out_shape,
        in_specs=[pl.BlockSpec(memory_space=pltpu.SMEM)] + [vmem] * len(arrays),
        out_specs=jax.tree.map(lambda _: vmem, out_shape),
        scratch_shapes=[pltpu.VMEM(shape, jnp.bfloat16) for shape in scratch],
        compiler_params=pltpu.CompilerParams(vmem_limit_bytes=16 * 1024 * 1024),
        cost_estimate=pl.CostEstimate(flops=flops, bytes_accessed=flops // 64, transcendentals=0),
    )(index, *arrays)


def body(features, tiles, scales, slots, live, times):
    count, width = tiles.shape[2], tiles.shape[4]
    slot_count = scales.shape[3]
    rim_count = max(1, count // 8)
    points = count * PB
    value = features.reshape(FEATURES, points)
    rim = value[:, : rim_count * PB]
    index = source_index(slots.reshape(count * slot_count), count, rim_count)
    image_shape = jax.ShapeDtypeStruct(value.shape, jnp.float32)
    rim_shape = jax.ShapeDtypeStruct(rim.shape, jnp.bfloat16)
    own_store = (count, FEATURES, LANES)
    rims_held = 2 * len(partners()) + 2
    far_store = (rims_held * rim_count + 1, FEATURES, LANES)
    pair_store = (rims_held * rim_count // 2 + 1, FEATURES, LANES)
    half = FEATURES * points * width
    scaled, near = call(
        first_kernel,
        (jax.ShapeDtypeStruct((points, width), jnp.bfloat16), image_shape),
        [own_store],
        half,
        index,
        value,
        tiles.reshape(points, width),
        scales.reshape(count, slot_count),
        live.reshape(count, 1),
    )
    times = times[:, None]
    total = value
    for step in range(1, TERMS + 1):
        rims, (scaled, near, total) = exchange(rim, (scaled, near, total))
        if step < TERMS:
            rim = call(rim_kernel, rim_shape, [pair_store], half // 8, index, *rims, scaled, near)
        last = step == TERMS
        out = call(
            functools.partial(far_kernel, step, last),
            jax.ShapeDtypeStruct(value.shape, jnp.bfloat16) if last else (image_shape,) * 2,
            [far_store] if last else [far_store, own_store],
            half if last else 2 * half,
            index,
            *rims,
            scaled,
            near,
            total,
            times,
        )
        if not last:
            total, near = out
    return out.reshape(features.shape)


def solution(mesh):
    return jax.shard_map(
        body,
        mesh=mesh,
        in_specs=(
            P(None, "gx", "gy", "gz"),
            P("gx", "gy", "gz", None, None),
            P("gx", "gy", "gz", None),
            P("gx", "gy", "gz", None),
            P("gx", "gy", "gz"),
            P(),
        ),
        out_specs=P(None, "gx", "gy", "gz"),
        check_vma=False,
    )
```

```python
import functools

import jax
import jax.numpy as jnp
from jax import lax
from jax.experimental import pallas as pl
from jax.experimental.pallas import tpu as pltpu
from jax.sharding import PartitionSpec as P

PB = 64
TERMS = 3
FEATURES = 64
NEAR = 4
PARTS = 4
LANES = 2 * PB
AXES = ("gx", "gy", "gz")


def pairings(count):
    first = [(i, i ^ 1) for i in range(count)]
    second = [(i, (i + 1) % count if i % 2 else (i - 1) % count) for i in range(count)]
    return [first] if count == 2 else [first, second]


def partner_rank(here, step, count):
    forward = jnp.where(here % 2 == 0, 1, 2)
    backward = 3 - forward
    rank = jnp.where(step == 1, 0, jnp.where(step == 2, forward, backward))
    there = here + step - 1
    return rank, (there >= 0) & (there < count)


def place(rank, here, count):
    there = here if rank == 0 else dict(pairings(count)[rank - 1])[here]
    return there if abs(there - here) <= 1 else None


def partners():
    x_count = len(pairings(lax.axis_size("gx"))) + 1
    y_count = len(pairings(lax.axis_size("gy"))) + 1
    pair_count = lax.axis_size("gz") // 2
    chips = [(x, b) for x in range(x_count) for b in range(pair_count)]
    side = [(x, y, b) for x, b in chips for y in range(1, y_count)]
    return side + [(x, 0, b) for x, b in chips[1:]]


def partner_number(x, y, b):
    x_count = len(pairings(lax.axis_size("gx"))) + 1
    y_count = len(pairings(lax.axis_size("gy"))) + 1
    pair_count = lax.axis_size("gz") // 2
    chip = x * pair_count + b
    return jnp.where(
        y > 0, chip * (y_count - 1) + y - 1, x_count * pair_count * (y_count - 1) + chip - 1
    )


def swap(value, by_core):
    sizes = [lax.axis_size(name) for name in AXES]
    pairs = []
    for i in range(sizes[0]):
        for j in range(sizes[1]):
            for k in range(sizes[2]):
                x, y, b = by_core[k % 2]
                to = (place(x, i, sizes[0]), place(y, j, sizes[1]), (k // 2 ^ b) * 2 + k % 2)
                if None in to:
                    to = (i, j, (k // 2 ^ 1) * 2 + k % 2)
                pairs.append(
                    ((i * sizes[1] + j) * sizes[2] + k, (to[0] * sizes[1] + to[1]) * sizes[2] + to[2])
                )
    return lax.ppermute(value, AXES, pairs)


def swap_cores(value):
    return lax.ppermute(value, "gz", [(k, k ^ 1) for k in range(lax.axis_size("gz"))])


def exchange(rim, work):
    chips = partners()
    alone = [swap(rim, (chips[-1], chips[-1]))] if len(chips) % 2 else []
    other = swap_cores(rim)
    both = jnp.stack([rim, other])
    steps = reversed(range(0, len(chips) - len(chips) % 2, 2))
    shares = [swap(both, (chips[t], chips[t + 1])) for t in steps]
    shares[1], *results = work(shares[1])
    received = jnp.concatenate(shares[::-1] + [panel[None] for panel in alone])
    return (received, swap_cores(received), other, rim), results


def source_index(slots, live, rim_count):
    count, slot_count = slots.shape
    layers = lax.axis_size("gz")
    x_at, y_at, z_at = (lax.axis_index(name) for name in AXES)
    rest = jnp.maximum(slots - count, 0)
    r = rest % rim_count
    m = (rest // rim_count) % layers
    c = (rest // (rim_count * layers)) % 3
    a = rest // (rim_count * layers * 3)
    x_rank, x_in = partner_rank(x_at, a, lax.axis_size("gx"))
    y_rank, y_in = partner_rank(y_at, c, lax.axis_size("gy"))
    flip = (m // 2) ^ (z_at // 2)
    chips = len(partners())
    core, target = z_at % 2, m % 2
    number = partner_number(x_rank, y_rank, flip)
    single = (number == chips - 1) if chips % 2 else jnp.zeros(number.shape, bool)
    holder = jnp.where(single, target, number % 2)
    panel = jnp.where(single, chips - 1, number // 2 * 2 + (target ^ holder))
    panel = panel + jnp.where(holder == core, 0, chips)
    here = (x_rank == 0) & (y_rank == 0) & (flip == 0)
    panel = jnp.where(here, 2 * chips + jnp.where(target == core, 1, 0), panel)
    zero = (2 * chips + 2) * rim_count
    far = jnp.where(x_in & y_in, panel * rim_count + r, zero)
    place = lax.broadcasted_iota(jnp.int32, slots.shape, 1)
    far = jnp.where(place < live, far, zero)
    index = jnp.where(place < NEAR, jnp.where(place < live, slots, count), far)
    index = index.reshape(count * slot_count)
    return index.astype(jnp.int32)


def left_half():
    return lax.broadcasted_iota(jnp.int32, (FEATURES, LANES), 1) < PB


def turn(pair):
    return jnp.concatenate([pair[:, PB:], pair[:, :PB]], axis=1)


def spread(pair, store, at):
    turned = turn(pair)
    store[at] = jnp.where(left_half(), pair, turned)
    store[at + 1] = jnp.where(left_half(), turned, pair)


def each_rim(rims, place_pair):
    mine_ref, others_ref, other_ref, own_ref = rims
    panels, _, rim = mine_ref.shape
    rim_count = rim // PB

    @pl.loop(0, panels)
    def _(panel):
        for t in range(rim // LANES):
            cut = slice(t * LANES, (t + 1) * LANES)
            at = panel * rim_count + 2 * t
            place_pair(mine_ref[panel, :, cut], at)
            place_pair(others_ref[panel, :, cut], at + panels * rim_count)

    for t in range(rim // LANES):
        cut = slice(t * LANES, (t + 1) * LANES)
        at = 2 * panels * rim_count + 2 * t
        place_pair(other_ref[:, cut], at)
        place_pair(own_ref[:, cut], at + rim_count)


def product(first, second, tile):
    both = lax.dot_general(
        jnp.concatenate([first, second], axis=0),
        tile,
        (((1,), (1,)), ((), ())),
        preferred_element_type=jnp.float32,
    )
    return jnp.where(left_half(), both[:FEATURES], both[FEATURES:])


def picked(store, index_ref, at):
    return jnp.concatenate(
        [
            jnp.where(left_half(), store[index_ref[at + k]], store[index_ref[at + k + 1]])
            for k in range(0, NEAR, 2)
        ],
        axis=1,
    )


def near_image(index_ref, store, tile_ref, near_out):
    slot_count = tile_ref.shape[1] // PB
    for t in range(near_out.shape[1] // LANES):
        at = pl.ds(t * LANES, LANES)
        near_out[:, at] = product(
            picked(store, index_ref, 2 * t * slot_count),
            picked(store, index_ref, (2 * t + 1) * slot_count),
            tile_ref[at, : NEAR * PB],
        )


def first_kernel(
    index_ref, _, value_hbm, raw_hbm, scale_hbm,
    __, tile_out, near_out, total_out,
    store, value_ref, raw_ref, scale_ref, arrived,
):
    count, slot_count = scale_ref.shape
    rows = raw_ref.shape[0] // PARTS
    fetches = [
        pltpu.make_async_copy(source, target, arrived.at[n])
        for n, (source, target) in enumerate(
            [(scale_hbm, scale_ref), (value_hbm, value_ref)]
            + [
                (raw_hbm.at[pl.ds(p * rows, rows)], raw_ref.at[pl.ds(p * rows, rows)])
                for p in range(PARTS)
            ]
        )
    ]
    for fetch in fetches:
        fetch.start()
    for fetch in fetches[:2]:
        fetch.wait()
    scales = scale_ref[...]
    lanes = jnp.concatenate(
        [jnp.broadcast_to(scales[:, k : k + 1], (count, PB)) for k in range(slot_count)], axis=1
    )
    for t in range(value_ref.shape[1] // LANES):
        pair = value_ref[:, t * LANES : (t + 1) * LANES]
        total_out[:, t * LANES : (t + 1) * LANES] = pair.astype(total_out.dtype)
        spread(pair, store, 2 * t)
    clear_last(store)
    for p in range(PARTS):
        fetches[2 + p].wait()
        for b in range(p * rows // PB, (p + 1) * rows // PB):
            at = pl.ds(b * PB, PB)
            scaled = raw_ref[at, :].astype(jnp.float32) * lanes[b : b + 1, :]
            tile_out[at, :] = scaled.astype(tile_out.dtype)
    near_image(index_ref, store, tile_out, near_out)


def clear_last(store):
    store[store.shape[0] - 1] = jnp.zeros(store.shape[1:], store.dtype)


def rim_kernel(index_ref, *refs):
    rims, (tile_ref, near_ref, rim_out, store) = refs[:4], refs[4:]
    slot_count = tile_ref.shape[1] // PB

    def keep(pair, number):
        store[number // 2] = pair

    each_rim(rims, keep)
    clear_last(store)

    def sources(row):
        base = row * slot_count + NEAR
        parts = []
        for k in range(0, NEAR, 2):
            halves = []
            for side in range(2):
                number = index_ref[base + k + side]
                pair = store[number // 2]
                halves.append(jnp.where(number % 2 == side, pair, turn(pair)))
            parts.append(jnp.where(left_half(), halves[0], halves[1]))
        return jnp.concatenate(parts, axis=1)

    for t in range(rim_out.shape[1] // LANES):
        at = pl.ds(t * LANES, LANES)
        far = product(sources(2 * t), sources(2 * t + 1), tile_ref[at, NEAR * PB :])
        rim_out[:, at] = (near_ref[:, at] + far).astype(rim_out.dtype)


def far_kernel(step, last, index_ref, *refs):
    if not last:
        refs = refs[1:]
    rims, (tile_ref, near_ref, total_ref, times_ref) = refs[:4], refs[4:8]
    if last:
        total_out, store = refs[8:]
    else:
        _, total_out, near_out, store, own_store = refs[8:]
        clear_last(own_store)
    slot_count = tile_ref.shape[1] // PB
    each_rim(rims, lambda pair, number: spread(pair, store, number))
    clear_last(store)
    factor = jnp.ones(times_ref.shape, jnp.float32)
    for n in range(1, step + 1):
        factor = factor * -times_ref[...] / jnp.float32(n)
    for t in range(near_ref.shape[1] // LANES):
        at = pl.ds(t * LANES, LANES)
        image = near_ref[:, at] + product(
            picked(store, index_ref, 2 * t * slot_count + NEAR),
            picked(store, index_ref, (2 * t + 1) * slot_count + NEAR),
            tile_ref[at, NEAR * PB :],
        )
        total = total_ref[:, at].astype(jnp.float32) + factor * image
        total_out[:, at] = total.astype(total_out.dtype)
        if not last:
            spread(image.astype(jnp.bfloat16), own_store, 2 * t)
    if not last:
        near_image(index_ref, own_store, tile_ref, near_out)


def call(kernel, out_shape, scratch, flops, index, *arrays, space=pltpu.VMEM, through=None):
    handed = () if through is None else (through,)
    out_shape = tuple(jax.ShapeDtypeStruct(x.shape, x.dtype) for x in handed) + out_shape
    return pl.pallas_call(
        kernel,
        out_shape=out_shape,
        in_specs=[pl.BlockSpec(memory_space=pltpu.SMEM)]
        + [pl.BlockSpec(memory_space=pl.ANY)] * len(handed)
        + [pl.BlockSpec(memory_space=space)] * len(arrays),
        out_specs=(pl.BlockSpec(memory_space=pl.ANY),) * len(handed)
        + (pl.BlockSpec(memory_space=pltpu.VMEM),) * (len(out_shape) - len(handed)),
        scratch_shapes=scratch,
        input_output_aliases={1: 0} if handed else {},
        compiler_params=pltpu.CompilerParams(vmem_limit_bytes=16 * 1024 * 1024),
        cost_estimate=pl.CostEstimate(flops=flops, bytes_accessed=flops // 64, transcendentals=0),
    )(index, *handed, *arrays)


def body(features, tiles, scales, slots, live, times):
    count, width = tiles.shape[2], tiles.shape[4]
    slot_count = scales.shape[3]
    rim_count = max(1, count // 8)
    points = count * PB
    value = features.reshape(FEATURES, points)
    rim = value[:, : rim_count * PB]
    index = source_index(slots.reshape(count, slot_count), live.reshape(count, 1), rim_count)
    rims_held = 2 * len(partners()) + 2
    half = FEATURES * points * width

    def blocks(number):
        return pltpu.VMEM((number, FEATURES, LANES), jnp.bfloat16)

    own_store = blocks(count + 1)
    far_store = blocks(rims_held * rim_count + 1)
    pair_store = blocks(rims_held * rim_count // 2 + 1)
    image_shape = jax.ShapeDtypeStruct(value.shape, jnp.float32)
    rim_shape = jax.ShapeDtypeStruct(rim.shape, jnp.bfloat16)
    tile_shape = jax.ShapeDtypeStruct((points, width), jnp.bfloat16)

    def first(through):
        return call(
            first_kernel,
            (tile_shape, image_shape, image_shape),
            [
                own_store,
                pltpu.VMEM(value.shape, jnp.bfloat16),
                pltpu.VMEM((points, width), jnp.bfloat16),
                pltpu.VMEM((count, slot_count), jnp.float32),
                pltpu.SemaphoreType.DMA((2 + PARTS,)),
            ],
            half,
            index,
            value,
            tiles.reshape(points, width),
            scales.reshape(count, slot_count),
            space=pltpu.HBM,
            through=through,
        )

    rims, (scaled, near, total) = exchange(rim, first)
    times = times[:, None]
    for step in range(1, TERMS):
        arrays = (index, *rims, scaled, near)
        (rim,) = call(rim_kernel, (rim_shape,), [pair_store], half // 8, *arrays)

        def rest(through):
            return call(
                functools.partial(far_kernel, step, False),
                (image_shape, image_shape),
                [far_store, own_store],
                2 * half,
                *arrays,
                total,
                times,
                through=through,
            )

        rims, (total, near) = exchange(rim, rest)
    (out,) = call(
        functools.partial(far_kernel, TERMS, True),
        (jax.ShapeDtypeStruct(value.shape, jnp.bfloat16),),
        [far_store],
        half,
        index,
        *rims,
        scaled,
        near,
        total,
        times,
    )
    return out.reshape(features.shape)


def solution(mesh):
    return jax.shard_map(
        body,
        mesh=mesh,
        in_specs=(
            P(None, "gx", "gy", "gz"),
            P("gx", "gy", "gz", None, None),
            P("gx", "gy", "gz", None),
            P("gx", "gy", "gz", None),
            P("gx", "gy", "gz"),
            P(),
        ),
        out_specs=P(None, "gx", "gy", "gz"),
        check_vma=False,
    )
```

```python
import functools

import jax
import jax.numpy as jnp
from jax import lax
from jax.experimental import pallas as pl
from jax.experimental.pallas import tpu as pltpu
from jax.sharding import PartitionSpec as P

PB = 64
TERMS = 3
FEATURES = 64
NEAR = 4
PARTS = 4
VMEM_MIB = 16
LANES = 2 * PB
AXES = ("gx", "gy", "gz")


def pairings(count):
    first = [(i, i ^ 1) for i in range(count)]
    second = [(i, (i + 1) % count if i % 2 else (i - 1) % count) for i in range(count)]
    return [first] if count == 2 else [first, second]


def partner_rank(here, step, count):
    forward = jnp.where(here % 2 == 0, 1, 2)
    backward = 3 - forward
    rank = jnp.where(step == 1, 0, jnp.where(step == 2, forward, backward))
    there = here + step - 1
    return rank, (there >= 0) & (there < count)


def place(rank, here, count):
    there = here if rank == 0 else dict(pairings(count)[rank - 1])[here]
    return there if abs(there - here) <= 1 else None


def partners():
    x_count = len(pairings(lax.axis_size("gx"))) + 1
    y_count = len(pairings(lax.axis_size("gy"))) + 1
    pair_count = lax.axis_size("gz") // 2
    chips = [(x, b) for x in range(x_count) for b in range(pair_count)]
    side = [(x, y, b) for x, b in chips for y in range(1, y_count)]
    return side + [(x, 0, b) for x, b in chips[1:]]


def partner_number(x, y, b):
    x_count = len(pairings(lax.axis_size("gx"))) + 1
    y_count = len(pairings(lax.axis_size("gy"))) + 1
    pair_count = lax.axis_size("gz") // 2
    chip = x * pair_count + b
    return jnp.where(
        y > 0, chip * (y_count - 1) + y - 1, x_count * pair_count * (y_count - 1) + chip - 1
    )


def swap(value, by_core):
    sizes = [lax.axis_size(name) for name in AXES]
    pairs = []
    for i in range(sizes[0]):
        for j in range(sizes[1]):
            for k in range(sizes[2]):
                x, y, b = by_core[k % 2]
                to = (place(x, i, sizes[0]), place(y, j, sizes[1]), (k // 2 ^ b) * 2 + k % 2)
                if None in to:
                    to = (i, j, (k // 2 ^ 1) * 2 + k % 2)
                pairs.append(
                    ((i * sizes[1] + j) * sizes[2] + k, (to[0] * sizes[1] + to[1]) * sizes[2] + to[2])
                )
    return lax.ppermute(value, AXES, pairs)


def swap_cores(value):
    return lax.ppermute(value, "gz", [(k, k ^ 1) for k in range(lax.axis_size("gz"))])


def exchange(rim, work):
    chips = partners()
    sides = len(pairings(lax.axis_size("gy")))
    plane = chips[-((len(chips) - sides) // (sides + 1)) :]
    other = swap_cores(rim)
    both = jnp.stack([rim, other])
    side = swap(both, (chips[0], chips[sides - 1]))
    alone = [swap(rim, (plane[-1], plane[-1]))] if len(plane) % 2 else []
    own = [
        swap(both, (plane[t], plane[t + 1])) for t in range(0, len(plane) - len(plane) % 2, 2)
    ]
    passed = [swap(side, (chip, chip)) for chip in plane[::-1]]
    passed[0], *results = work(passed[0])
    received = jnp.concatenate([side] + passed[::-1] + own + [panel[None] for panel in alone])
    return (received, swap_cores(received), other, rim), results


def source_index(slots, live, rim_count):
    count, slot_count = slots.shape
    layers = lax.axis_size("gz")
    x_at, y_at, z_at = (lax.axis_index(name) for name in AXES)
    rest = jnp.maximum(slots - count, 0)
    r = rest % rim_count
    m = (rest // rim_count) % layers
    c = (rest // (rim_count * layers)) % 3
    a = rest // (rim_count * layers * 3)
    x_rank, x_in = partner_rank(x_at, a, lax.axis_size("gx"))
    y_rank, y_in = partner_rank(y_at, c, lax.axis_size("gy"))
    flip = (m // 2) ^ (z_at // 2)
    chips = len(partners())
    core, target = z_at % 2, m % 2
    number = partner_number(x_rank, y_rank, flip)
    single = (number == chips - 1) if chips % 2 else jnp.zeros(number.shape, bool)
    holder = jnp.where(single, target, number % 2)
    panel = jnp.where(single, chips - 1, number // 2 * 2 + (target ^ holder))
    panel = panel + jnp.where(holder == core, 0, chips)
    here = (x_rank == 0) & (y_rank == 0) & (flip == 0)
    panel = jnp.where(here, 2 * chips + jnp.where(target == core, 1, 0), panel)
    zero = (2 * chips + 2) * rim_count
    far = jnp.where(x_in & y_in, panel * rim_count + r, zero)
    place = lax.broadcasted_iota(jnp.int32, slots.shape, 1)
    far = jnp.where(place < live, far, zero)
    index = jnp.where(place < NEAR, jnp.where(place < live, slots, count), far)
    index = index.reshape(count * slot_count)
    return index.astype(jnp.int32)


def left_half():
    return lax.broadcasted_iota(jnp.int32, (FEATURES, LANES), 1) < PB


def turn(pair):
    return jnp.concatenate([pair[:, PB:], pair[:, :PB]], axis=1)


def spread(pair, store, at):
    turned = turn(pair)
    store[at] = jnp.where(left_half(), pair, turned)
    store[at + 1] = jnp.where(left_half(), turned, pair)


def each_rim(rims, place_pair):
    mine_ref, others_ref, other_ref, own_ref = rims
    panels, _, rim = mine_ref.shape
    rim_count = rim // PB

    @pl.loop(0, panels)
    def _(panel):
        for t in range(rim // LANES):
            cut = slice(t * LANES, (t + 1) * LANES)
            at = panel * rim_count + 2 * t
            place_pair(mine_ref[panel, :, cut], at)
            place_pair(others_ref[panel, :, cut], at + panels * rim_count)

    for t in range(rim // LANES):
        cut = slice(t * LANES, (t + 1) * LANES)
        at = 2 * panels * rim_count + 2 * t
        place_pair(other_ref[:, cut], at)
        place_pair(own_ref[:, cut], at + rim_count)


def product(first, second, tile):
    both = lax.dot_general(
        jnp.concatenate([first, second], axis=0),
        tile,
        (((1,), (1,)), ((), ())),
        preferred_element_type=jnp.float32,
    )
    return jnp.where(left_half(), both[:FEATURES], both[FEATURES:])


def picked(store, index_ref, at):
    return jnp.concatenate(
        [
            jnp.where(left_half(), store[index_ref[at + k]], store[index_ref[at + k + 1]])
            for k in range(0, NEAR, 2)
        ],
        axis=1,
    )


def near_image(index_ref, store, tile_ref, near_out):
    slot_count = tile_ref.shape[1] // PB
    for t in range(near_out.shape[1] // LANES):
        at = pl.ds(t * LANES, LANES)
        near_out[:, at] = product(
            picked(store, index_ref, 2 * t * slot_count),
            picked(store, index_ref, (2 * t + 1) * slot_count),
            tile_ref[at, : NEAR * PB],
        )


def first_kernel(
    index_ref, _, value_hbm, raw_hbm, scale_hbm,
    __, tile_out, near_out,
    store, value_ref, raw_ref, scale_ref, arrived,
):
    count, slot_count = scale_ref.shape
    rows = raw_ref.shape[0] // PARTS
    fetches = [
        pltpu.make_async_copy(source, target, arrived.at[n])
        for n, (source, target) in enumerate(
            [(scale_hbm, scale_ref), (value_hbm, value_ref)]
            + [
                (raw_hbm.at[pl.ds(p * rows, rows)], raw_ref.at[pl.ds(p * rows, rows)])
                for p in range(PARTS)
            ]
        )
    ]
    for fetch in fetches:
        fetch.start()
    for fetch in fetches[:2]:
        fetch.wait()
    scales = scale_ref[...]
    lanes = jnp.concatenate(
        [jnp.broadcast_to(scales[:, k : k + 1], (count, PB)) for k in range(slot_count)], axis=1
    )
    for t in range(value_ref.shape[1] // LANES):
        pair = value_ref[:, t * LANES : (t + 1) * LANES]
        spread(pair, store, 2 * t)
    clear_last(store)
    for p in range(PARTS):
        fetches[2 + p].wait()
        for b in range(p * rows // PB, (p + 1) * rows // PB):
            at = pl.ds(b * PB, PB)
            scaled = raw_ref[at, :].astype(jnp.float32) * lanes[b : b + 1, :]
            tile_out[at, :] = scaled.astype(tile_out.dtype)
    near_image(index_ref, store, tile_out, near_out)


def clear_last(store):
    store[store.shape[0] - 1] = jnp.zeros(store.shape[1:], store.dtype)


def rim_kernel(index_ref, *refs):
    rims, (tile_ref, near_ref, rim_out, store) = refs[:4], refs[4:]
    slot_count = tile_ref.shape[1] // PB

    def keep(pair, number):
        store[number // 2] = pair

    each_rim(rims, keep)
    clear_last(store)

    def sources(row):
        base = row * slot_count + NEAR
        parts = []
        for k in range(0, NEAR, 2):
            halves = []
            for side in range(2):
                number = index_ref[base + k + side]
                pair = store[number // 2]
                halves.append(jnp.where(number % 2 == side, pair, turn(pair)))
            parts.append(jnp.where(left_half(), halves[0], halves[1]))
        return jnp.concatenate(parts, axis=1)

    for t in range(rim_out.shape[1] // LANES):
        at = pl.ds(t * LANES, LANES)
        far = product(sources(2 * t), sources(2 * t + 1), tile_ref[at, NEAR * PB :])
        rim_out[:, at] = (near_ref[:, at] + far).astype(rim_out.dtype)


def far_kernel(step, last, index_ref, *refs):
    if not last:
        refs = refs[1:]
    rims, (tile_ref, near_ref, times_ref, total_ref) = refs[:4], refs[4:8]
    if last:
        total_out, store = refs[8:]
    else:
        _, total_out, near_out, store, own_store, *fetching = refs[8:]
        clear_last(own_store)
        if fetching:
            features_hbm, (total_ref, arrived) = total_ref, fetching
            fetch = pltpu.make_async_copy(features_hbm, total_ref, arrived)
            fetch.start()
    slot_count = tile_ref.shape[1] // PB
    each_rim(rims, lambda pair, number: spread(pair, store, number))
    clear_last(store)
    if not last and fetching:
        fetch.wait()
    factor = jnp.ones(times_ref.shape, jnp.float32)
    for n in range(1, step + 1):
        factor = factor * -times_ref[...] / jnp.float32(n)
    for t in range(near_ref.shape[1] // LANES):
        at = pl.ds(t * LANES, LANES)
        image = near_ref[:, at] + product(
            picked(store, index_ref, 2 * t * slot_count + NEAR),
            picked(store, index_ref, (2 * t + 1) * slot_count + NEAR),
            tile_ref[at, NEAR * PB :],
        )
        total = total_ref[:, at].astype(jnp.float32) + factor * image
        total_out[:, at] = total.astype(total_out.dtype)
        if not last:
            spread(image.astype(jnp.bfloat16), own_store, 2 * t)
    if not last:
        near_image(index_ref, own_store, tile_ref, near_out)


def call(kernel, out_shape, scratch, flops, index, *arrays, fetched=(), through=None):
    handed = () if through is None else (through,)
    out_shape = tuple(jax.ShapeDtypeStruct(x.shape, x.dtype) for x in handed) + out_shape
    anywhere, vmem = pl.BlockSpec(memory_space=pl.ANY), pl.BlockSpec(memory_space=pltpu.VMEM)
    fetched = [pltpu.with_memory_space_constraint(x, pltpu.HBM) for x in fetched]
    return pl.pallas_call(
        kernel,
        out_shape=out_shape,
        in_specs=[pl.BlockSpec(memory_space=pltpu.SMEM)]
        + [anywhere] * len(handed)
        + [vmem] * len(arrays)
        + [pl.BlockSpec(memory_space=pltpu.HBM)] * len(fetched),
        out_specs=(anywhere,) * len(handed) + (vmem,) * (len(out_shape) - len(handed)),
        scratch_shapes=scratch,
        input_output_aliases={1: 0} if handed else {},
        compiler_params=pltpu.CompilerParams(vmem_limit_bytes=VMEM_MIB * 1024 * 1024),
        cost_estimate=pl.CostEstimate(flops=flops, bytes_accessed=flops // 64, transcendentals=0),
    )(index, *handed, *arrays, *fetched)


def body(features, tiles, scales, slots, live, times):
    count, width = tiles.shape[2], tiles.shape[4]
    slot_count = scales.shape[3]
    rim_count = max(1, count // 8)
    points = count * PB
    value = features.reshape(FEATURES, points)
    rim = value[:, : rim_count * PB]
    index = source_index(slots.reshape(count, slot_count), live.reshape(count, 1), rim_count)
    rims_held = 2 * len(partners()) + 2
    half = FEATURES * points * width

    def blocks(number):
        return pltpu.VMEM((number, FEATURES, LANES), jnp.bfloat16)

    own_store = blocks(count + 1)
    far_store = blocks(rims_held * rim_count + 1)
    pair_store = blocks(rims_held * rim_count // 2 + 1)
    image_shape = jax.ShapeDtypeStruct(value.shape, jnp.float32)
    rim_shape = jax.ShapeDtypeStruct(rim.shape, jnp.bfloat16)
    tile_shape = jax.ShapeDtypeStruct((points, width), jnp.bfloat16)

    def first(through):
        return call(
            first_kernel,
            (tile_shape, image_shape),
            [
                own_store,
                pltpu.VMEM(value.shape, jnp.bfloat16),
                pltpu.VMEM((points, width), jnp.bfloat16),
                pltpu.VMEM((count, slot_count), jnp.float32),
                pltpu.SemaphoreType.DMA((2 + PARTS,)),
            ],
            half,
            index,
            fetched=(value, tiles.reshape(points, width), scales.reshape(count, slot_count)),
            through=through,
        )

    rims, (scaled, near) = exchange(rim, first)
    times = times[:, None]
    for step in range(1, TERMS):
        arrays = (index, *rims, scaled, near)
        (rim,) = call(rim_kernel, (rim_shape,), [pair_store], half // 8, *arrays)

        def rest(through):
            begun = step > 1
            fetch = [pltpu.VMEM(value.shape, jnp.bfloat16), pltpu.SemaphoreType.DMA]
            return call(
                functools.partial(far_kernel, step, False),
                (image_shape, image_shape),
                [far_store, own_store] + ([] if begun else fetch),
                2 * half,
                *arrays,
                times,
                *([total] if begun else []),
                fetched=() if begun else (value,),
                through=through,
            )

        rims, (total, near) = exchange(rim, rest)
    (out,) = call(
        functools.partial(far_kernel, TERMS, True),
        (jax.ShapeDtypeStruct(value.shape, jnp.bfloat16),),
        [far_store],
        half,
        index,
        *rims,
        scaled,
        near,
        times,
        total,
    )
    return out.reshape(features.shape)


def solution(mesh):
    return jax.shard_map(
        body,
        mesh=mesh,
        in_specs=(
            P(None, "gx", "gy", "gz"),
            P("gx", "gy", "gz", None, None),
            P("gx", "gy", "gz", None),
            P("gx", "gy", "gz", None),
            P("gx", "gy", "gz"),
            P(),
        ),
        out_specs=P(None, "gx", "gy", "gz"),
        check_vma=False,
    )
```

```python
import functools

import jax
import jax.numpy as jnp
from jax import lax
from jax.experimental import pallas as pl
from jax.experimental.pallas import tpu as pltpu
from jax.sharding import PartitionSpec as P

PB = 64
TERMS = 3
FEATURES = 64
NEAR = 4
PARTS = 4
VMEM_MIB = 16
LANES = 2 * PB
AXES = ("gx", "gy", "gz")


def pairings(count):
    first = [(i, i ^ 1) for i in range(count)]
    second = [(i, (i + 1) % count if i % 2 else (i - 1) % count) for i in range(count)]
    return [first] if count == 2 else [first, second]


def partner_rank(here, step, count):
    forward = jnp.where((here & 1) == 0, 1, 2)
    backward = 3 - forward
    rank = jnp.where(step == 1, 0, jnp.where(step == 2, forward, backward))
    there = here + step - 1
    return rank, (there >= 0) & (there < count)


def place(rank, here, count):
    there = here if rank == 0 else dict(pairings(count)[rank - 1])[here]
    return there if abs(there - here) <= 1 else None


def partners():
    x_count = len(pairings(lax.axis_size("gx"))) + 1
    y_count = len(pairings(lax.axis_size("gy"))) + 1
    pair_count = lax.axis_size("gz") // 2
    chips = [(x, b) for x in range(x_count) for b in range(pair_count)]
    side = [(x, y, b) for x, b in chips for y in range(1, y_count)]
    return side + [(x, 0, b) for x, b in chips[1:]]


def partner_number(x, y, b):
    x_count = len(pairings(lax.axis_size("gx"))) + 1
    y_count = len(pairings(lax.axis_size("gy"))) + 1
    pair_count = lax.axis_size("gz") // 2
    chip = x * pair_count + b
    return jnp.where(
        y > 0, chip * (y_count - 1) + y - 1, x_count * pair_count * (y_count - 1) + chip - 1
    )


def swap(value, by_core):
    sizes = [lax.axis_size(name) for name in AXES]
    pairs = []
    for i in range(sizes[0]):
        for j in range(sizes[1]):
            for k in range(sizes[2]):
                x, y, b = by_core[k % 2]
                to = (place(x, i, sizes[0]), place(y, j, sizes[1]), (k // 2 ^ b) * 2 + k % 2)
                if None in to:
                    to = (i, j, (k // 2 ^ 1) * 2 + k % 2)
                pairs.append(
                    ((i * sizes[1] + j) * sizes[2] + k, (to[0] * sizes[1] + to[1]) * sizes[2] + to[2])
                )
    return lax.ppermute(value, AXES, pairs)


def swap_cores(value):
    return lax.ppermute(value, "gz", [(k, k ^ 1) for k in range(lax.axis_size("gz"))])


def exchange(rim, work):
    chips = partners()
    sides = len(pairings(lax.axis_size("gy")))
    plane = chips[-((len(chips) - sides) // (sides + 1)) :]
    other = swap_cores(rim)
    both = jnp.stack([rim, other])
    side = swap(both, (chips[0], chips[sides - 1]))
    alone = [swap(rim, (plane[-1], plane[-1]))] if len(plane) % 2 else []
    own = [
        swap(both, (plane[t], plane[t + 1])) for t in range(0, len(plane) - len(plane) % 2, 2)
    ]
    passed = [swap(side, (chip, chip)) for chip in plane[::-1]]
    own[0], *results = work(own[0])
    received = jnp.concatenate([side] + passed[::-1] + own + [panel[None] for panel in alone])
    return (received, swap_cores(received), other, rim), results


def source_index(slots, live, count, rim_count):
    layers = lax.axis_size("gz")
    x_at, y_at, z_at = (lax.axis_index(name) for name in AXES)
    rest = jnp.maximum(slots - count, 0)
    column = sum((rest >= rim_count * layers * n).astype(jnp.int32) for n in range(1, 9))
    a = (column >= 3).astype(jnp.int32) + (column >= 6).astype(jnp.int32)
    c = column - 3 * a
    inside = rest - rim_count * layers * column
    m = sum((inside >= rim_count * n).astype(jnp.int32) for n in range(1, layers))
    r = inside - rim_count * m
    x_rank, x_in = partner_rank(x_at, a, lax.axis_size("gx"))
    y_rank, y_in = partner_rank(y_at, c, lax.axis_size("gy"))
    flip = (m >> 1) ^ (z_at >> 1)
    chips = len(partners())
    core, target = z_at & 1, m & 1
    number = partner_number(x_rank, y_rank, flip)
    holder, panel = number & 1, (number & -2) + (target ^ (number & 1))
    if chips % 2:
        holder = jnp.where(number == chips - 1, target, holder)
        panel = jnp.where(number == chips - 1, chips - 1, panel)
    panel = panel + jnp.where(holder == core, 0, chips)
    here = (x_rank == 0) & (y_rank == 0) & (flip == 0)
    panel = jnp.where(here, 2 * chips + jnp.where(target == core, 1, 0), panel)
    zero = (2 * chips + 2) * rim_count
    place = lax.broadcasted_iota(jnp.int32, slots.shape, 0)
    used = place < live
    far = jnp.where(x_in & y_in & used, panel * rim_count + r, zero)
    return jnp.where(place < NEAR, jnp.where(used, slots, count), far)


def left_half():
    return lax.broadcasted_iota(jnp.int32, (FEATURES, LANES), 1) < PB


def turn(pair):
    return jnp.concatenate([pair[:, PB:], pair[:, :PB]], axis=1)


def spread(pair, store, at):
    turned = turn(pair)
    store[at] = jnp.where(left_half(), pair, turned)
    store[at + 1] = jnp.where(left_half(), turned, pair)


def each_rim(rims, place_pair):
    mine_ref, others_ref, other_ref, own_ref = rims
    panels, _, rim = mine_ref.shape
    rim_count = rim // PB

    @pl.loop(0, panels)
    def _(panel):
        for t in range(rim // LANES):
            cut = slice(t * LANES, (t + 1) * LANES)
            at = panel * rim_count + 2 * t
            place_pair(mine_ref[panel, :, cut], at)
            place_pair(others_ref[panel, :, cut], at + panels * rim_count)

    for t in range(rim // LANES):
        cut = slice(t * LANES, (t + 1) * LANES)
        at = 2 * panels * rim_count + 2 * t
        place_pair(other_ref[:, cut], at)
        place_pair(own_ref[:, cut], at + rim_count)


def product(first, second, tile):
    both = lax.dot_general(
        jnp.concatenate([first, second], axis=0),
        tile,
        (((1,), (1,)), ((), ())),
        preferred_element_type=jnp.float32,
    )
    return jnp.where(left_half(), both[:FEATURES], both[FEATURES:])


def picked(store, index_ref, first, row):
    return jnp.concatenate(
        [
            jnp.where(left_half(), store[index_ref[k, row]], store[index_ref[k + 1, row]])
            for k in range(first, first + NEAR, 2)
        ],
        axis=1,
    )


def fold_kernel(
    _, raw_hbm, slot_hbm, live_hbm, scale_hbm,
    __, tile_out, index_out,
    raw_ref, slot_ref, live_ref, scale_ref, arrived, *, rim_count,
):
    count = slot_ref.shape[1]
    rows = raw_ref.shape[0] // PARTS
    fetches = [
        pltpu.make_async_copy(source, target, arrived.at[n])
        for n, (source, target) in enumerate(
            [(scale_hbm, scale_ref), (slot_hbm, slot_ref), (live_hbm, live_ref)]
            + [
                (raw_hbm.at[pl.ds(p * rows, rows)], raw_ref.at[pl.ds(p * rows, rows)])
                for p in range(PARTS)
            ]
        )
    ]
    for fetch in fetches:
        fetch.start()
    half = lax.broadcasted_iota(jnp.int32, (PB, LANES), 1) < PB
    for fetch in fetches[:3]:
        fetch.wait()
    index_out[...] = source_index(slot_ref[...], live_ref[...], count, rim_count)
    for p in range(PARTS):
        fetches[3 + p].wait()
        for b in range(p * rows // PB, (p + 1) * rows // PB):
            for k in range(0, scale_ref.shape[0], 2):
                at = pl.ds(b * PB, PB), pl.ds(k * PB, LANES)
                scale = jnp.where(half, scale_ref[k, b], scale_ref[k + 1, b])
                tile_out[at] = (raw_ref[at].astype(jnp.float32) * scale).astype(tile_out.dtype)


def near_kernel(index_ref, value_ref, tile_ref, near_out, store):
    for t in range(value_ref.shape[1] // LANES):
        spread(value_ref[:, t * LANES : (t + 1) * LANES], store, 2 * t)
    clear_last(store)
    for t in range(near_out.shape[1] // LANES):
        at = pl.ds(t * LANES, LANES)
        near_out[:, at] = product(
            picked(store, index_ref, 0, 2 * t),
            picked(store, index_ref, 0, 2 * t + 1),
            tile_ref[at, : NEAR * PB],
        )


def clear_last(store):
    store[store.shape[0] - 1] = jnp.zeros(store.shape[1:], store.dtype)


def rim_kernel(index_ref, *refs):
    rims, (tile_ref, near_ref, rim_out, store) = refs[:4], refs[4:]

    def keep(pair, number):
        store[number // 2] = pair

    each_rim(rims, keep)
    clear_last(store)

    def sources(row):
        parts = []
        for k in range(NEAR, 2 * NEAR, 2):
            halves = []
            for side in range(2):
                number = index_ref[k + side, row]
                pair = store[number >> 1]
                halves.append(jnp.where((number & 1) == side, pair, turn(pair)))
            parts.append(jnp.where(left_half(), halves[0], halves[1]))
        return jnp.concatenate(parts, axis=1)

    for t in range(rim_out.shape[1] // LANES):
        at = pl.ds(t * LANES, LANES)
        far = product(sources(2 * t), sources(2 * t + 1), tile_ref[at, NEAR * PB :])
        rim_out[:, at] = (near_ref[:, at] + far).astype(rim_out.dtype)


def far_kernel(step, last, index_ref, *refs):
    if not last:
        refs = refs[1:]
    rims, (tile_ref, near_ref, times_ref, total_ref) = refs[:4], refs[4:8]
    if last:
        result_hbm, store, total_out, sent = refs[8:]
    else:
        _, total_out, value_out, store, *fetching = refs[8:]
        if fetching:
            features_hbm, (total_ref, arrived) = total_ref, fetching
            fetch = pltpu.make_async_copy(features_hbm, total_ref, arrived)
            fetch.start()
    each_rim(rims, lambda pair, number: spread(pair, store, number))
    clear_last(store)
    if not last and fetching:
        fetch.wait()
    factor = jnp.ones(times_ref.shape, jnp.float32)
    for n in range(1, step + 1):
        factor = factor * -times_ref[...] / jnp.float32(n)
    pairs = near_ref.shape[1] // LANES
    sends = []
    for t in range(pairs):
        at = pl.ds(t * LANES, LANES)
        image = near_ref[:, at] + product(
            picked(store, index_ref, NEAR, 2 * t),
            picked(store, index_ref, NEAR, 2 * t + 1),
            tile_ref[at, NEAR * PB :],
        )
        total = total_ref[:, at].astype(jnp.float32) + factor * image
        total_out[:, at] = total.astype(total_out.dtype)
        if not last:
            value_out[:, at] = image.astype(value_out.dtype)
        elif (t + 1) % (pairs // PARTS) == 0:
            part = pl.ds((t + 1 - pairs // PARTS) * LANES, pairs // PARTS * LANES)
            send = pltpu.make_async_copy(
                total_out.at[:, part], result_hbm.at[:, part], sent.at[len(sends)]
            )
            send.start()
            sends.append(send)
    for send in sends:
        send.wait()


def call(kernel, results, scratch, flops, index, *arrays, fetched=(), through=None, to_hbm=False):
    scalars = () if index is None else (index,)
    handed = () if through is None else (through,)
    out_shape = tuple(jax.ShapeDtypeStruct(x.shape, x.dtype) for x in handed) + results
    anywhere, vmem = pl.BlockSpec(memory_space=pl.ANY), pl.BlockSpec(memory_space=pltpu.VMEM)
    hbm = pl.BlockSpec(memory_space=pltpu.HBM)
    fetched = [pltpu.with_memory_space_constraint(x, pltpu.HBM) for x in fetched]
    return pl.pallas_call(
        kernel,
        out_shape=out_shape,
        in_specs=[pl.BlockSpec(memory_space=pltpu.SMEM)] * len(scalars)
        + [anywhere] * len(handed)
        + [vmem] * len(arrays)
        + [hbm] * len(fetched),
        out_specs=(anywhere,) * len(handed) + (hbm if to_hbm else vmem,) * len(results),
        scratch_shapes=scratch,
        input_output_aliases={len(scalars): 0} if handed else {},
        compiler_params=pltpu.CompilerParams(vmem_limit_bytes=VMEM_MIB * 1024 * 1024),
        cost_estimate=pl.CostEstimate(flops=flops, bytes_accessed=flops // 64, transcendentals=0),
    )(*scalars, *handed, *arrays, *fetched)


def body(features, tiles, scales, slots, live, times):
    count, width = tiles.shape[2], tiles.shape[4]
    slot_count = scales.shape[3]
    rim_count = max(1, count // 8)
    points = count * PB
    value = features.reshape(FEATURES, points)
    rim = value[:, : rim_count * PB]
    scales = scales.reshape(count, slot_count).T
    slots = slots.reshape(count, slot_count).T
    rims_held = 2 * len(partners()) + 2
    half = FEATURES * points * width

    def blocks(number):
        return pltpu.VMEM((number, FEATURES, LANES), jnp.bfloat16)

    own_store = blocks(count + 1)
    far_store = blocks(rims_held * rim_count + 1)
    pair_store = blocks(rims_held * rim_count // 2 + 1)
    image_shape = jax.ShapeDtypeStruct(value.shape, jnp.float32)
    value_shape = jax.ShapeDtypeStruct(value.shape, jnp.bfloat16)
    rim_shape = jax.ShapeDtypeStruct(rim.shape, jnp.bfloat16)
    tile_shape = jax.ShapeDtypeStruct((points, width), jnp.bfloat16)
    index_shape = jax.ShapeDtypeStruct(slots.shape, jnp.int32)

    def fold(through):
        return call(
            functools.partial(fold_kernel, rim_count=rim_count),
            (tile_shape, index_shape),
            [
                pltpu.VMEM((points, width), jnp.bfloat16),
                pltpu.VMEM(slots.shape, jnp.int32),
                pltpu.VMEM((1, count), jnp.int32),
                pltpu.SMEM(scales.shape, jnp.float32),
                pltpu.SemaphoreType.DMA((PARTS + 3,)),
            ],
            half,
            None,
            fetched=(tiles.reshape(points, width), slots, live.reshape(1, count), scales),
            through=through,
        )

    rims, (scaled, index) = exchange(rim, fold)
    (near,) = call(near_kernel, (image_shape,), [own_store], half, index, value, scaled)
    times = times[:, None]
    total = value
    for step in range(1, TERMS):
        arrays = (index, *rims, scaled, near)
        (rim,) = call(rim_kernel, (rim_shape,), [pair_store], half // 8, *arrays)

        def rest(through):
            begun = step > 1
            fetch = [pltpu.VMEM(value.shape, jnp.bfloat16), pltpu.SemaphoreType.DMA]
            return call(
                functools.partial(far_kernel, step, False),
                (image_shape, value_shape),
                [far_store] + ([] if begun else fetch),
                half,
                *arrays,
                times,
                *([total] if begun else []),
                fetched=() if begun else (value,),
                through=through,
            )

        rims, (total, value) = exchange(rim, rest)
        (near,) = call(near_kernel, (image_shape,), [own_store], half, index, value, scaled)
    (out,) = call(
        functools.partial(far_kernel, TERMS, True),
        (value_shape,),
        [
            far_store,
            pltpu.VMEM(value.shape, jnp.bfloat16),
            pltpu.SemaphoreType.DMA((PARTS,)),
        ],
        half,
        index,
        *rims,
        scaled,
        near,
        times,
        total,
        to_hbm=True,
    )
    return out.reshape(features.shape)


def solution(mesh):
    return jax.shard_map(
        body,
        mesh=mesh,
        in_specs=(
            P(None, "gx", "gy", "gz"),
            P("gx", "gy", "gz", None, None),
            P("gx", "gy", "gz", None),
            P("gx", "gy", "gz", None),
            P("gx", "gy", "gz"),
            P(),
        ),
        out_specs=P(None, "gx", "gy", "gz"),
        check_vma=False,
    )
```

```python
import functools

import jax
import jax.numpy as jnp
from jax import lax
from jax.experimental import pallas as pl
from jax.experimental.pallas import tpu as pltpu
from jax.sharding import PartitionSpec as P

PB = 64
TERMS = 3
FEATURES = 64
NEAR = 4
PARTS = 4
VMEM_MIB = 16
LANES = 2 * PB
AXES = ("gx", "gy", "gz")


def pairings(count):
    first = [(i, i ^ 1) for i in range(count)]
    second = [(i, (i + 1) % count if i % 2 else (i - 1) % count) for i in range(count)]
    return [first] if count == 2 else [first, second]


def partner_rank(here, step, count):
    forward = jnp.where((here & 1) == 0, 1, 2)
    backward = 3 - forward
    rank = jnp.where(step == 1, 0, jnp.where(step == 2, forward, backward))
    there = here + step - 1
    return rank, (there >= 0) & (there < count)


def place(rank, here, count):
    there = here if rank == 0 else dict(pairings(count)[rank - 1])[here]
    return there if abs(there - here) <= 1 else None


def partners():
    x_count = len(pairings(lax.axis_size("gx"))) + 1
    y_count = len(pairings(lax.axis_size("gy"))) + 1
    pair_count = lax.axis_size("gz") // 2
    chips = [(x, b) for x in range(x_count) for b in range(pair_count)]
    side = [(x, y, b) for x, b in chips for y in range(1, y_count)]
    return side + [(x, 0, b) for x, b in chips[1:]]


def partner_number(x, y, b):
    x_count = len(pairings(lax.axis_size("gx"))) + 1
    y_count = len(pairings(lax.axis_size("gy"))) + 1
    pair_count = lax.axis_size("gz") // 2
    chip = x * pair_count + b
    return jnp.where(
        y > 0, chip * (y_count - 1) + y - 1, x_count * pair_count * (y_count - 1) + chip - 1
    )


def swap(value, by_core):
    sizes = [lax.axis_size(name) for name in AXES]
    pairs = []
    for i in range(sizes[0]):
        for j in range(sizes[1]):
            for k in range(sizes[2]):
                x, y, b = by_core[k % 2]
                to = (place(x, i, sizes[0]), place(y, j, sizes[1]), (k // 2 ^ b) * 2 + k % 2)
                if None in to:
                    to = (i, j, (k // 2 ^ 1) * 2 + k % 2)
                pairs.append(
                    ((i * sizes[1] + j) * sizes[2] + k, (to[0] * sizes[1] + to[1]) * sizes[2] + to[2])
                )
    return lax.ppermute(value, AXES, pairs)


def swap_cores(value):
    return lax.ppermute(value, "gz", [(k, k ^ 1) for k in range(lax.axis_size("gz"))])


def exchange(rim, work):
    chips = partners()
    sides = len(pairings(lax.axis_size("gy")))
    plane = chips[-((len(chips) - sides) // (sides + 1)) :]
    other = swap_cores(rim)
    both = jnp.stack([rim, other])
    side = swap(both, (chips[0], chips[sides - 1]))
    alone = [swap(rim, (plane[-1], plane[-1]))] if len(plane) % 2 else []
    own = [
        swap(both, (plane[t], plane[t + 1])) for t in range(0, len(plane) - len(plane) % 2, 2)
    ]
    passed = [swap(side, (chip, chip)) for chip in plane[::-1]]
    own[0], *results = work(own[0])
    received = jnp.concatenate([side] + passed[::-1] + own + [panel[None] for panel in alone])
    return (received, swap_cores(received), other, rim), results


def source_index(slots, live, count, rim_count):
    layers = lax.axis_size("gz")
    x_at, y_at, z_at = (lax.axis_index(name) for name in AXES)
    rest = jnp.maximum(slots - count, 0)
    column = sum((rest >= rim_count * layers * n).astype(jnp.int32) for n in range(1, 9))
    a = (column >= 3).astype(jnp.int32) + (column >= 6).astype(jnp.int32)
    c = column - 3 * a
    inside = rest - rim_count * layers * column
    m = sum((inside >= rim_count * n).astype(jnp.int32) for n in range(1, layers))
    r = inside - rim_count * m
    x_rank, x_in = partner_rank(x_at, a, lax.axis_size("gx"))
    y_rank, y_in = partner_rank(y_at, c, lax.axis_size("gy"))
    flip = (m >> 1) ^ (z_at >> 1)
    chips = len(partners())
    core, target = z_at & 1, m & 1
    number = partner_number(x_rank, y_rank, flip)
    holder, panel = number & 1, (number & -2) + (target ^ (number & 1))
    if chips % 2:
        holder = jnp.where(number == chips - 1, target, holder)
        panel = jnp.where(number == chips - 1, chips - 1, panel)
    panel = panel + jnp.where(holder == core, 0, chips)
    here = (x_rank == 0) & (y_rank == 0) & (flip == 0)
    panel = jnp.where(here, 2 * chips + jnp.where(target == core, 1, 0), panel)
    zero = (2 * chips + 2) * rim_count
    place = lax.broadcasted_iota(jnp.int32, slots.shape, 0)
    used = place < live
    far = jnp.where(x_in & y_in & used, panel * rim_count + r, zero)
    return jnp.where(place < NEAR, jnp.where(used, slots, count), far)


def left_half():
    return lax.broadcasted_iota(jnp.int32, (FEATURES, LANES), 1) < PB


def turn(pair):
    return jnp.concatenate([pair[:, PB:], pair[:, :PB]], axis=1)


def spread(pair, store, at):
    turned = turn(pair)
    store[at] = jnp.where(left_half(), pair, turned)
    store[at + 1] = jnp.where(left_half(), turned, pair)


def each_rim(rims, place_pair):
    mine_ref, others_ref, other_ref, own_ref = rims
    panels, _, rim = mine_ref.shape
    rim_count = rim // PB

    @pl.loop(0, panels)
    def _(panel):
        for t in range(rim // LANES):
            cut = slice(t * LANES, (t + 1) * LANES)
            at = panel * rim_count + 2 * t
            place_pair(mine_ref[panel, :, cut], at)
            place_pair(others_ref[panel, :, cut], at + panels * rim_count)

    for t in range(rim // LANES):
        cut = slice(t * LANES, (t + 1) * LANES)
        at = 2 * panels * rim_count + 2 * t
        place_pair(other_ref[:, cut], at)
        place_pair(own_ref[:, cut], at + rim_count)


def product(first, second, tile):
    both = lax.dot_general(
        jnp.concatenate([first, second], axis=0),
        tile,
        (((1,), (1,)), ((), ())),
        preferred_element_type=jnp.float32,
    )
    return jnp.where(left_half(), both[:FEATURES], both[FEATURES:])


def picked(store, index_ref, first, row):
    return jnp.concatenate(
        [
            jnp.where(left_half(), store[index_ref[k, row]], store[index_ref[k + 1, row]])
            for k in range(first, first + NEAR, 2)
        ],
        axis=1,
    )


def fold_kernel(
    _, raw_hbm, slot_hbm, live_hbm, scale_hbm, time_hbm,
    __, tile_out, index_out, time_out,
    raw_ref, slot_ref, live_ref, scale_ref, time_ref, arrived, *, rim_count,
):
    count = slot_ref.shape[1]
    rows = raw_ref.shape[0] // PARTS
    fetches = [
        pltpu.make_async_copy(source, target, arrived.at[n])
        for n, (source, target) in enumerate(
            [(scale_hbm, scale_ref), (slot_hbm, slot_ref), (live_hbm, live_ref), (time_hbm, time_ref)]
            + [
                (raw_hbm.at[pl.ds(p * rows, rows)], raw_ref.at[pl.ds(p * rows, rows)])
                for p in range(PARTS)
            ]
        )
    ]
    for fetch in fetches:
        fetch.start()
    half = lax.broadcasted_iota(jnp.int32, (PB, LANES), 1) < PB
    small = len(fetches) - PARTS
    for fetch in fetches[:small]:
        fetch.wait()
    eye = [lax.broadcasted_iota(jnp.int32, (FEATURES, FEATURES), n) for n in range(2)]
    column = jnp.where(eye[0] == eye[1], time_ref[...], 0.0)
    time_out[...] = jnp.sum(column, axis=1, keepdims=True)
    index_out[...] = source_index(slot_ref[...], live_ref[...], count, rim_count)
    for p in range(PARTS):
        fetches[small + p].wait()
        for b in range(p * rows // PB, (p + 1) * rows // PB):
            for k in range(0, scale_ref.shape[0], 2):
                at = pl.ds(b * PB, PB), pl.ds(k * PB, LANES)
                scale = jnp.where(half, scale_ref[k, b], scale_ref[k + 1, b])
                tile_out[at] = (raw_ref[at].astype(jnp.float32) * scale).astype(tile_out.dtype)


def near_kernel(index_ref, value_ref, tile_ref, near_out, store):
    for t in range(value_ref.shape[1] // LANES):
        spread(value_ref[:, t * LANES : (t + 1) * LANES], store, 2 * t)
    clear_last(store)
    for t in range(near_out.shape[1] // LANES):
        at = pl.ds(t * LANES, LANES)
        near_out[:, at] = product(
            picked(store, index_ref, 0, 2 * t),
            picked(store, index_ref, 0, 2 * t + 1),
            tile_ref[at, : NEAR * PB],
        )


def clear_last(store):
    store[store.shape[0] - 1] = jnp.zeros(store.shape[1:], store.dtype)


def rim_kernel(index_ref, *refs):
    rims, (tile_ref, near_ref, rim_out, store) = refs[:4], refs[4:]

    def keep(pair, number):
        store[number // 2] = pair

    each_rim(rims, keep)
    clear_last(store)

    def sources(row):
        parts = []
        for k in range(NEAR, 2 * NEAR, 2):
            halves = []
            for side in range(2):
                number = index_ref[k + side, row]
                pair = store[number >> 1]
                halves.append(jnp.where((number & 1) == side, pair, turn(pair)))
            parts.append(jnp.where(left_half(), halves[0], halves[1]))
        return jnp.concatenate(parts, axis=1)

    for t in range(rim_out.shape[1] // LANES):
        at = pl.ds(t * LANES, LANES)
        far = product(sources(2 * t), sources(2 * t + 1), tile_ref[at, NEAR * PB :])
        rim_out[:, at] = (near_ref[:, at] + far).astype(rim_out.dtype)


def far_kernel(step, last, index_ref, *refs):
    if not last:
        refs = refs[1:]
    rims, (tile_ref, near_ref, times_ref, total_ref) = refs[:4], refs[4:8]
    if last:
        result_hbm, store, total_out, sent = refs[8:]
    else:
        _, total_out, value_out, store, *fetching = refs[8:]
        if fetching:
            features_hbm, (total_ref, arrived) = total_ref, fetching
            fetch = pltpu.make_async_copy(features_hbm, total_ref, arrived)
            fetch.start()
    each_rim(rims, lambda pair, number: spread(pair, store, number))
    clear_last(store)
    if not last and fetching:
        fetch.wait()
    factor = jnp.ones(times_ref.shape, jnp.float32)
    for n in range(1, step + 1):
        factor = factor * -times_ref[...] / jnp.float32(n)
    pairs = near_ref.shape[1] // LANES
    sends = []
    for t in range(pairs):
        at = pl.ds(t * LANES, LANES)
        image = near_ref[:, at] + product(
            picked(store, index_ref, NEAR, 2 * t),
            picked(store, index_ref, NEAR, 2 * t + 1),
            tile_ref[at, NEAR * PB :],
        )
        total = total_ref[:, at].astype(jnp.float32) + factor * image
        total_out[:, at] = total.astype(total_out.dtype)
        if not last:
            value_out[:, at] = image.astype(value_out.dtype)
        elif (t + 1) % (pairs // PARTS) == 0:
            part = pl.ds((t + 1 - pairs // PARTS) * LANES, pairs // PARTS * LANES)
            send = pltpu.make_async_copy(
                total_out.at[:, part], result_hbm.at[:, part], sent.at[len(sends)]
            )
            send.start()
            sends.append(send)
    for send in sends:
        send.wait()


def call(kernel, results, scratch, flops, index, *arrays, fetched=(), through=None, to_hbm=False):
    scalars = () if index is None else (index,)
    handed = () if through is None else (through,)
    out_shape = tuple(jax.ShapeDtypeStruct(x.shape, x.dtype) for x in handed) + results
    anywhere, vmem = pl.BlockSpec(memory_space=pl.ANY), pl.BlockSpec(memory_space=pltpu.VMEM)
    hbm = pl.BlockSpec(memory_space=pltpu.HBM)
    fetched = [pltpu.with_memory_space_constraint(x, pltpu.HBM) for x in fetched]
    return pl.pallas_call(
        kernel,
        out_shape=out_shape,
        in_specs=[pl.BlockSpec(memory_space=pltpu.SMEM)] * len(scalars)
        + [anywhere] * len(handed)
        + [vmem] * len(arrays)
        + [hbm] * len(fetched),
        out_specs=(anywhere,) * len(handed) + (hbm if to_hbm else vmem,) * len(results),
        scratch_shapes=scratch,
        input_output_aliases={len(scalars): 0} if handed else {},
        compiler_params=pltpu.CompilerParams(vmem_limit_bytes=VMEM_MIB * 1024 * 1024),
        cost_estimate=pl.CostEstimate(flops=flops, bytes_accessed=flops // 64, transcendentals=0),
    )(*scalars, *handed, *arrays, *fetched)


def body(features, tiles, scales, slots, live, times):
    count, width = tiles.shape[2], tiles.shape[4]
    slot_count = scales.shape[3]
    rim_count = max(1, count // 8)
    points = count * PB
    value = features.reshape(FEATURES, points)
    rim = value[:, : rim_count * PB]
    scales = scales.reshape(count, slot_count).T
    slots = slots.reshape(count, slot_count).T
    rims_held = 2 * len(partners()) + 2
    half = FEATURES * points * width

    def blocks(number):
        return pltpu.VMEM((number, FEATURES, LANES), jnp.bfloat16)

    own_store = blocks(count + 1)
    far_store = blocks(rims_held * rim_count + 1)
    pair_store = blocks(rims_held * rim_count // 2 + 1)
    image_shape = jax.ShapeDtypeStruct(value.shape, jnp.float32)
    value_shape = jax.ShapeDtypeStruct(value.shape, jnp.bfloat16)
    rim_shape = jax.ShapeDtypeStruct(rim.shape, jnp.bfloat16)
    tile_shape = jax.ShapeDtypeStruct((points, width), jnp.bfloat16)
    index_shape = jax.ShapeDtypeStruct(slots.shape, jnp.int32)

    def fold(through):
        return call(
            functools.partial(fold_kernel, rim_count=rim_count),
            (tile_shape, index_shape, jax.ShapeDtypeStruct((FEATURES, 1), jnp.float32)),
            [
                pltpu.VMEM((points, width), jnp.bfloat16),
                pltpu.VMEM(slots.shape, jnp.int32),
                pltpu.VMEM((1, count), jnp.int32),
                pltpu.SMEM(scales.shape, jnp.float32),
                pltpu.VMEM((1, FEATURES), jnp.float32),
                pltpu.SemaphoreType.DMA((PARTS + 4,)),
            ],
            half,
            None,
            fetched=(
                tiles.reshape(points, width),
                slots,
                live.reshape(1, count),
                scales,
                times.reshape(1, FEATURES),
            ),
            through=through,
        )

    rims, (scaled, index, times) = exchange(rim, fold)
    (near,) = call(near_kernel, (image_shape,), [own_store], half, index, value, scaled)
    total = value
    for step in range(1, TERMS):
        arrays = (index, *rims, scaled, near)
        (rim,) = call(rim_kernel, (rim_shape,), [pair_store], half // 8, *arrays)

        def rest(through):
            begun = step > 1
            fetch = [pltpu.VMEM(value.shape, jnp.bfloat16), pltpu.SemaphoreType.DMA]
            return call(
                functools.partial(far_kernel, step, False),
                (image_shape, value_shape),
                [far_store] + ([] if begun else fetch),
                half,
                *arrays,
                times,
                *([total] if begun else []),
                fetched=() if begun else (value,),
                through=through,
            )

        rims, (total, value) = exchange(rim, rest)
        (near,) = call(near_kernel, (image_shape,), [own_store], half, index, value, scaled)
    (out,) = call(
        functools.partial(far_kernel, TERMS, True),
        (value_shape,),
        [
            far_store,
            pltpu.VMEM(value.shape, jnp.bfloat16),
            pltpu.SemaphoreType.DMA((PARTS,)),
        ],
        half,
        index,
        *rims,
        scaled,
        near,
        times,
        total,
        to_hbm=True,
    )
    return out.reshape(features.shape)


def solution(mesh):
    return jax.shard_map(
        body,
        mesh=mesh,
        in_specs=(
            P(None, "gx", "gy", "gz"),
            P("gx", "gy", "gz", None, None),
            P("gx", "gy", "gz", None),
            P("gx", "gy", "gz", None),
            P("gx", "gy", "gz"),
            P(),
        ),
        out_specs=P(None, "gx", "gy", "gz"),
        check_vma=False,
    )
```

```python
import functools

import jax
import jax.numpy as jnp
from jax import lax
from jax.experimental import pallas as pl
from jax.experimental.pallas import tpu as pltpu
from jax.sharding import PartitionSpec as P

PB = 64
TERMS = 3
FEATURES = 64
NEAR = 4
PARTS = 4
VMEM_MIB = 16
LANES = 2 * PB
AXES = ("gx", "gy", "gz")


def pairings(count):
    first = [(i, i ^ 1) for i in range(count)]
    second = [(i, (i + 1) % count if i % 2 else (i - 1) % count) for i in range(count)]
    return [first] if count == 2 else [first, second]


def partner_rank(here, step, count):
    forward = jnp.where((here & 1) == 0, 1, 2)
    backward = 3 - forward
    rank = jnp.where(step == 1, 0, jnp.where(step == 2, forward, backward))
    there = here + step - 1
    return rank, (there >= 0) & (there < count)


def place(rank, here, count):
    there = here if rank == 0 else dict(pairings(count)[rank - 1])[here]
    return there if abs(there - here) <= 1 else None


def partners():
    x_count = len(pairings(lax.axis_size("gx"))) + 1
    y_count = len(pairings(lax.axis_size("gy"))) + 1
    pair_count = lax.axis_size("gz") // 2
    chips = [(x, b) for x in range(x_count) for b in range(pair_count)]
    side = [(x, y, b) for x, b in chips for y in range(1, y_count)]
    return side + [(x, 0, b) for x, b in chips[1:]]


def partner_number(x, y, b):
    x_count = len(pairings(lax.axis_size("gx"))) + 1
    y_count = len(pairings(lax.axis_size("gy"))) + 1
    pair_count = lax.axis_size("gz") // 2
    chip = x * pair_count + b
    return jnp.where(
        y > 0, chip * (y_count - 1) + y - 1, x_count * pair_count * (y_count - 1) + chip - 1
    )


def swap(value, by_core):
    sizes = [lax.axis_size(name) for name in AXES]
    pairs = []
    for i in range(sizes[0]):
        for j in range(sizes[1]):
            for k in range(sizes[2]):
                x, y, b = by_core[k % 2]
                to = (place(x, i, sizes[0]), place(y, j, sizes[1]), (k // 2 ^ b) * 2 + k % 2)
                if None in to:
                    to = (i, j, (k // 2 ^ 1) * 2 + k % 2)
                pairs.append(
                    ((i * sizes[1] + j) * sizes[2] + k, (to[0] * sizes[1] + to[1]) * sizes[2] + to[2])
                )
    return lax.ppermute(value, AXES, pairs)


def swap_cores(value):
    return lax.ppermute(value, "gz", [(k, k ^ 1) for k in range(lax.axis_size("gz"))])


def exchange(rim, work):
    chips = partners()
    sides = len(pairings(lax.axis_size("gy")))
    plane = chips[-((len(chips) - sides) // (sides + 1)) :]
    other = swap_cores(rim)
    both = jnp.stack([rim, other])
    side = swap(both, (chips[0], chips[sides - 1]))
    alone = [swap(rim, (plane[-1], plane[-1]))] if len(plane) % 2 else []
    own = [
        swap(both, (plane[t], plane[t + 1])) for t in range(0, len(plane) - len(plane) % 2, 2)
    ]
    passed = [swap(side, (chip, chip)) for chip in plane[::-1]]
    own[0], *results = work(own[0])
    received = jnp.concatenate([side] + passed[::-1] + own + [panel[None] for panel in alone])
    return (received, swap_cores(received), other, rim), results


def source_index(slots, live, count, rim_count):
    layers = lax.axis_size("gz")
    x_at, y_at, z_at = (lax.axis_index(name) for name in AXES)
    rest = jnp.maximum(slots - count, 0)
    column = sum((rest >= rim_count * layers * n).astype(jnp.int32) for n in range(1, 9))
    a = (column >= 3).astype(jnp.int32) + (column >= 6).astype(jnp.int32)
    c = column - 3 * a
    inside = rest - rim_count * layers * column
    m = sum((inside >= rim_count * n).astype(jnp.int32) for n in range(1, layers))
    r = inside - rim_count * m
    x_rank, x_in = partner_rank(x_at, a, lax.axis_size("gx"))
    y_rank, y_in = partner_rank(y_at, c, lax.axis_size("gy"))
    flip = (m >> 1) ^ (z_at >> 1)
    chips = len(partners())
    core, target = z_at & 1, m & 1
    number = partner_number(x_rank, y_rank, flip)
    holder, panel = number & 1, (number & -2) + (target ^ (number & 1))
    if chips % 2:
        holder = jnp.where(number == chips - 1, target, holder)
        panel = jnp.where(number == chips - 1, chips - 1, panel)
    panel = panel + jnp.where(holder == core, 0, chips)
    here = (x_rank == 0) & (y_rank == 0) & (flip == 0)
    panel = jnp.where(here, 2 * chips + jnp.where(target == core, 1, 0), panel)
    zero = (2 * chips + 2) * rim_count
    place = lax.broadcasted_iota(jnp.int32, slots.shape, 0)
    used = place < live
    far = jnp.where(x_in & y_in & used, panel * rim_count + r, zero)
    return jnp.where(place < NEAR, jnp.where(used, slots, count), far)


def left_half():
    return lax.broadcasted_iota(jnp.int32, (FEATURES, LANES), 1) < PB


def turn(pair):
    return jnp.concatenate([pair[:, PB:], pair[:, :PB]], axis=1)


def spread(pair, store, at):
    turned = turn(pair)
    store[at] = jnp.where(left_half(), pair, turned)
    store[at + 1] = jnp.where(left_half(), turned, pair)


def each_rim(rims, place_pair):
    mine_ref, others_ref, other_ref, own_ref = rims
    panels, _, rim = mine_ref.shape
    rim_count = rim // PB

    for panel in range(panels):
        for t in range(rim // LANES):
            cut = slice(t * LANES, (t + 1) * LANES)
            at = panel * rim_count + 2 * t
            place_pair(mine_ref[panel, :, cut], at)
            place_pair(others_ref[panel, :, cut], at + panels * rim_count)

    for t in range(rim // LANES):
        cut = slice(t * LANES, (t + 1) * LANES)
        at = 2 * panels * rim_count + 2 * t
        place_pair(other_ref[:, cut], at)
        place_pair(own_ref[:, cut], at + rim_count)


def product(first, second, tile):
    both = lax.dot_general(
        jnp.concatenate([first, second], axis=0),
        tile,
        (((1,), (1,)), ((), ())),
        preferred_element_type=jnp.float32,
    )
    return jnp.where(left_half(), both[:FEATURES], both[FEATURES:])


def picked(store, index_ref, first, row):
    return jnp.concatenate(
        [
            jnp.where(left_half(), store[index_ref[k, row]], store[index_ref[k + 1, row]])
            for k in range(first, first + NEAR, 2)
        ],
        axis=1,
    )


def fold_kernel(
    _, raw_hbm, slot_hbm, live_hbm, scale_hbm, time_hbm,
    __, tile_out, index_out, time_out,
    raw_ref, slot_ref, live_ref, scale_ref, time_ref, arrived, *, rim_count,
):
    count = slot_ref.shape[1]
    rows = raw_ref.shape[0] // PARTS
    fetches = [
        pltpu.make_async_copy(source, target, arrived.at[n])
        for n, (source, target) in enumerate(
            [(scale_hbm, scale_ref), (slot_hbm, slot_ref), (live_hbm, live_ref), (time_hbm, time_ref)]
            + [
                (raw_hbm.at[pl.ds(p * rows, rows)], raw_ref.at[pl.ds(p * rows, rows)])
                for p in range(PARTS)
            ]
        )
    ]
    for fetch in fetches:
        fetch.start()
    half = lax.broadcasted_iota(jnp.int32, (PB, LANES), 1) < PB
    small = len(fetches) - PARTS
    for fetch in fetches[:small]:
        fetch.wait()
    eye = [lax.broadcasted_iota(jnp.int32, (FEATURES, FEATURES), n) for n in range(2)]
    column = jnp.where(eye[0] == eye[1], time_ref[...], 0.0)
    time_out[...] = jnp.sum(column, axis=1, keepdims=True)
    index_out[...] = source_index(slot_ref[...], live_ref[...], count, rim_count)
    for p in range(PARTS):
        fetches[small + p].wait()
        for b in range(p * rows // PB, (p + 1) * rows // PB):
            for k in range(0, scale_ref.shape[0], 2):
                at = pl.ds(b * PB, PB), pl.ds(k * PB, LANES)
                scale = jnp.where(half, scale_ref[k, b], scale_ref[k + 1, b])
                tile_out[at] = (raw_ref[at].astype(jnp.float32) * scale).astype(tile_out.dtype)


def near_kernel(index_ref, value_ref, tile_ref, near_out, store):
    for t in range(value_ref.shape[1] // LANES):
        spread(value_ref[:, t * LANES : (t + 1) * LANES], store, 2 * t)
    clear_last(store)
    for t in range(near_out.shape[1] // LANES):
        at = pl.ds(t * LANES, LANES)
        near_out[:, at] = product(
            picked(store, index_ref, 0, 2 * t),
            picked(store, index_ref, 0, 2 * t + 1),
            tile_ref[at, : NEAR * PB],
        )


def clear_last(store):
    store[store.shape[0] - 1] = jnp.zeros(store.shape[1:], store.dtype)


def rim_kernel(index_ref, *refs):
    rims, (tile_ref, near_ref, rim_out, store) = refs[:4], refs[4:]

    def keep(pair, number):
        store[number // 2] = pair

    each_rim(rims, keep)
    clear_last(store)

    def sources(row):
        parts = []
        for k in range(NEAR, 2 * NEAR, 2):
            halves = []
            for side in range(2):
                number = index_ref[k + side, row]
                pair = store[number >> 1]
                halves.append(jnp.where((number & 1) == side, pair, turn(pair)))
            parts.append(jnp.where(left_half(), halves[0], halves[1]))
        return jnp.concatenate(parts, axis=1)

    for t in range(rim_out.shape[1] // LANES):
        at = pl.ds(t * LANES, LANES)
        far = product(sources(2 * t), sources(2 * t + 1), tile_ref[at, NEAR * PB :])
        rim_out[:, at] = (near_ref[:, at] + far).astype(rim_out.dtype)


def far_kernel(step, last, index_ref, *refs):
    if not last:
        refs = refs[1:]
    rims, (tile_ref, near_ref, times_ref, total_ref) = refs[:4], refs[4:8]
    if last:
        result_hbm, store, total_out, sent = refs[8:]
    else:
        _, total_out, value_out, store, *fetching = refs[8:]
        if fetching:
            features_hbm, (total_ref, arrived) = total_ref, fetching
            fetch = pltpu.make_async_copy(features_hbm, total_ref, arrived)
            fetch.start()
    each_rim(rims, lambda pair, number: spread(pair, store, number))
    clear_last(store)
    if not last and fetching:
        fetch.wait()
    factor = jnp.ones(times_ref.shape, jnp.float32)
    for n in range(1, step + 1):
        factor = factor * -times_ref[...] / jnp.float32(n)
    pairs = near_ref.shape[1] // LANES
    sends = []
    for t in range(pairs):
        at = pl.ds(t * LANES, LANES)
        image = near_ref[:, at] + product(
            picked(store, index_ref, NEAR, 2 * t),
            picked(store, index_ref, NEAR, 2 * t + 1),
            tile_ref[at, NEAR * PB :],
        )
        total = total_ref[:, at].astype(jnp.float32) + factor * image
        total_out[:, at] = total.astype(total_out.dtype)
        if not last:
            value_out[:, at] = image.astype(value_out.dtype)
        elif (t + 1) % (pairs // PARTS) == 0:
            part = pl.ds((t + 1 - pairs // PARTS) * LANES, pairs // PARTS * LANES)
            send = pltpu.make_async_copy(
                total_out.at[:, part], result_hbm.at[:, part], sent.at[len(sends)]
            )
            send.start()
            sends.append(send)
    for send in sends:
        send.wait()


def call(kernel, results, scratch, flops, index, *arrays, fetched=(), through=None, to_hbm=False):
    scalars = () if index is None else (index,)
    handed = () if through is None else (through,)
    out_shape = tuple(jax.ShapeDtypeStruct(x.shape, x.dtype) for x in handed) + results
    anywhere, vmem = pl.BlockSpec(memory_space=pl.ANY), pl.BlockSpec(memory_space=pltpu.VMEM)
    hbm = pl.BlockSpec(memory_space=pltpu.HBM)
    fetched = [pltpu.with_memory_space_constraint(x, pltpu.HBM) for x in fetched]
    return pl.pallas_call(
        kernel,
        out_shape=out_shape,
        in_specs=[pl.BlockSpec(memory_space=pltpu.SMEM)] * len(scalars)
        + [anywhere] * len(handed)
        + [vmem] * len(arrays)
        + [hbm] * len(fetched),
        out_specs=(anywhere,) * len(handed) + (hbm if to_hbm else vmem,) * len(results),
        scratch_shapes=scratch,
        input_output_aliases={len(scalars): 0} if handed else {},
        compiler_params=pltpu.CompilerParams(vmem_limit_bytes=VMEM_MIB * 1024 * 1024),
        cost_estimate=pl.CostEstimate(flops=flops, bytes_accessed=flops // 64, transcendentals=0),
    )(*scalars, *handed, *arrays, *fetched)


def body(features, tiles, scales, slots, live, times):
    count, width = tiles.shape[2], tiles.shape[4]
    slot_count = scales.shape[3]
    rim_count = max(1, count // 8)
    points = count * PB
    value = features.reshape(FEATURES, points)
    rim = value[:, : rim_count * PB]
    scales = scales.reshape(count, slot_count).T
    slots = slots.reshape(count, slot_count).T
    rims_held = 2 * len(partners()) + 2
    half = FEATURES * points * width

    def blocks(number):
        return pltpu.VMEM((number, FEATURES, LANES), jnp.bfloat16)

    own_store = blocks(count + 1)
    far_store = blocks(rims_held * rim_count + 1)
    pair_store = blocks(rims_held * rim_count // 2 + 1)
    image_shape = jax.ShapeDtypeStruct(value.shape, jnp.float32)
    value_shape = jax.ShapeDtypeStruct(value.shape, jnp.bfloat16)
    rim_shape = jax.ShapeDtypeStruct(rim.shape, jnp.bfloat16)
    tile_shape = jax.ShapeDtypeStruct((points, width), jnp.bfloat16)
    index_shape = jax.ShapeDtypeStruct(slots.shape, jnp.int32)

    def fold(through):
        return call(
            functools.partial(fold_kernel, rim_count=rim_count),
            (tile_shape, index_shape, jax.ShapeDtypeStruct((FEATURES, 1), jnp.float32)),
            [
                pltpu.VMEM((points, width), jnp.bfloat16),
                pltpu.VMEM(slots.shape, jnp.int32),
                pltpu.VMEM((1, count), jnp.int32),
                pltpu.SMEM(scales.shape, jnp.float32),
                pltpu.VMEM((1, FEATURES), jnp.float32),
                pltpu.SemaphoreType.DMA((PARTS + 4,)),
            ],
            half,
            None,
            fetched=(
                tiles.reshape(points, width),
                slots,
                live.reshape(1, count),
                scales,
                times.reshape(1, FEATURES),
            ),
            through=through,
        )

    rims, (scaled, index, times) = exchange(rim, fold)
    (near,) = call(near_kernel, (image_shape,), [own_store], half, index, value, scaled)
    total = value
    for step in range(1, TERMS):
        arrays = (index, *rims, scaled, near)
        (rim,) = call(rim_kernel, (rim_shape,), [pair_store], half // 8, *arrays)

        def rest(through):
            begun = step > 1
            fetch = [pltpu.VMEM(value.shape, jnp.bfloat16), pltpu.SemaphoreType.DMA]
            return call(
                functools.partial(far_kernel, step, False),
                (image_shape, value_shape),
                [far_store] + ([] if begun else fetch),
                half,
                *arrays,
                times,
                *([total] if begun else []),
                fetched=() if begun else (value,),
                through=through,
            )

        rims, (total, value) = exchange(rim, rest)
        (near,) = call(near_kernel, (image_shape,), [own_store], half, index, value, scaled)
    (out,) = call(
        functools.partial(far_kernel, TERMS, True),
        (value_shape,),
        [
            far_store,
            pltpu.VMEM(value.shape, jnp.bfloat16),
            pltpu.SemaphoreType.DMA((PARTS,)),
        ],
        half,
        index,
        *rims,
        scaled,
        near,
        times,
        total,
        to_hbm=True,
    )
    return out.reshape(features.shape)


def solution(mesh):
    return jax.shard_map(
        body,
        mesh=mesh,
        in_specs=(
            P(None, "gx", "gy", "gz"),
            P("gx", "gy", "gz", None, None),
            P("gx", "gy", "gz", None),
            P("gx", "gy", "gz", None),
            P("gx", "gy", "gz"),
            P(),
        ),
        out_specs=P(None, "gx", "gy", "gz"),
        check_vma=False,
    )
```

```python
import functools

import jax
import jax.numpy as jnp
from jax import lax
from jax.experimental import pallas as pl
from jax.experimental.pallas import tpu as pltpu
from jax.sharding import PartitionSpec as P

PB = 64
TERMS = 3
FEATURES = 64
NEAR = 4
PARTS = 4
VMEM_MIB = 16
LANES = 2 * PB
AXES = ("gx", "gy", "gz")


def pairings(count):
    first = [(i, i ^ 1) for i in range(count)]
    second = [(i, (i + 1) % count if i % 2 else (i - 1) % count) for i in range(count)]
    return [first] if count == 2 else [first, second]


def partner_rank(here, step, count):
    forward = jnp.where((here & 1) == 0, 1, 2)
    backward = 3 - forward
    rank = jnp.where(step == 1, 0, jnp.where(step == 2, forward, backward))
    there = here + step - 1
    return rank, (there >= 0) & (there < count)


def place(rank, here, count):
    there = here if rank == 0 else dict(pairings(count)[rank - 1])[here]
    return there if abs(there - here) <= 1 else None


def partners():
    x_count = len(pairings(lax.axis_size("gx"))) + 1
    y_count = len(pairings(lax.axis_size("gy"))) + 1
    pair_count = lax.axis_size("gz") // 2
    chips = [(x, b) for x in range(x_count) for b in range(pair_count)]
    side = [(x, y, b) for x, b in chips for y in range(1, y_count)]
    return side + [(x, 0, b) for x, b in chips[1:]]


def partner_number(x, y, b):
    x_count = len(pairings(lax.axis_size("gx"))) + 1
    y_count = len(pairings(lax.axis_size("gy"))) + 1
    pair_count = lax.axis_size("gz") // 2
    chip = x * pair_count + b
    return jnp.where(
        y > 0, chip * (y_count - 1) + y - 1, x_count * pair_count * (y_count - 1) + chip - 1
    )


def swap(value, by_core):
    sizes = [lax.axis_size(name) for name in AXES]
    pairs = []
    for i in range(sizes[0]):
        for j in range(sizes[1]):
            for k in range(sizes[2]):
                x, y, b = by_core[k % 2]
                to = (place(x, i, sizes[0]), place(y, j, sizes[1]), (k // 2 ^ b) * 2 + k % 2)
                if None in to:
                    to = (i, j, (k // 2 ^ 1) * 2 + k % 2)
                pairs.append(
                    ((i * sizes[1] + j) * sizes[2] + k, (to[0] * sizes[1] + to[1]) * sizes[2] + to[2])
                )
    return lax.ppermute(value, AXES, pairs)


def swap_cores(value):
    return lax.ppermute(value, "gz", [(k, k ^ 1) for k in range(lax.axis_size("gz"))])


def exchange(both, work, far_first):
    chips = partners()
    sides = len(pairings(lax.axis_size("gy")))
    plane = chips[-((len(chips) - sides) // (sides + 1)) :]
    rim = both[0]
    side = swap(both, (chips[0], chips[sides - 1]))
    alone = [swap(rim, (plane[-1], plane[-1]))] if len(plane) % 2 else []
    own = [
        swap(both, (plane[t], plane[t + 1])) for t in range(0, len(plane) - len(plane) % 2, 2)
    ]
    step = -1 if far_first else 1
    passed = [swap(side, (chip, chip)) for chip in plane[::step]]
    passed[0], *results = work(passed[0])
    received = jnp.concatenate([side] + passed[::step] + own + [panel[None] for panel in alone])
    return received, results


def source_index(slots, live, count, rim_count):
    layers = lax.axis_size("gz")
    x_at, y_at, z_at = (lax.axis_index(name) for name in AXES)
    rest = jnp.maximum(slots - count, 0)
    column = sum((rest >= rim_count * layers * n).astype(jnp.int32) for n in range(1, 9))
    a = (column >= 3).astype(jnp.int32) + (column >= 6).astype(jnp.int32)
    c = column - 3 * a
    inside = rest - rim_count * layers * column
    m = sum((inside >= rim_count * n).astype(jnp.int32) for n in range(1, layers))
    r = inside - rim_count * m
    x_rank, x_in = partner_rank(x_at, a, lax.axis_size("gx"))
    y_rank, y_in = partner_rank(y_at, c, lax.axis_size("gy"))
    flip = (m >> 1) ^ (z_at >> 1)
    chips = len(partners())
    core, target = z_at & 1, m & 1
    number = partner_number(x_rank, y_rank, flip)
    holder, panel = number & 1, (number & -2) + (target ^ (number & 1))
    if chips % 2:
        holder = jnp.where(number == chips - 1, target, holder)
        panel = jnp.where(number == chips - 1, chips - 1, panel)
    here = (x_rank == 0) & (y_rank == 0) & (flip == 0)
    place = lax.broadcasted_iota(jnp.int32, slots.shape, 0)
    used = place < live
    there = x_in & y_in & used
    all_rims = jnp.where(
        here,
        2 * chips + jnp.where(target == core, 1, 0),
        panel + jnp.where(holder == core, 0, chips),
    )
    far = jnp.where(there, all_rims * rim_count + r, (2 * chips + 2) * rim_count)
    index = jnp.where(place < NEAR, jnp.where(used, slots, count), far)
    held = jnp.where(here, chips, panel) * rim_count + r
    holder = jnp.where(here, target, holder)
    zero = (chips + 1) * rim_count
    return index, *(jnp.where(there & (holder == at), held, zero) for at in (core, 1 - core))


def left_half():
    return lax.broadcasted_iota(jnp.int32, (FEATURES, LANES), 1) < PB


def turn(pair):
    return jnp.concatenate([pair[:, PB:], pair[:, :PB]], axis=1)


def spread(pair, store, at):
    turned = turn(pair)
    store[at] = jnp.where(left_half(), pair, turned)
    store[at + 1] = jnp.where(left_half(), turned, pair)


def each_pair(panels_ref, first, place_pair):
    rim = panels_ref.shape[2]
    for panel in range(panels_ref.shape[0]):
        for t in range(rim // LANES):
            place_pair(
                panels_ref[panel, :, t * LANES : (t + 1) * LANES],
                first + panel * (rim // PB) + 2 * t,
            )


def product(first, second, tile):
    both = lax.dot_general(
        jnp.concatenate([first, second], axis=0),
        tile,
        (((1,), (1,)), ((), ())),
        preferred_element_type=jnp.float32,
    )
    return jnp.where(left_half(), both[:FEATURES], both[FEATURES:])


def picked(store, index_ref, first, row):
    return jnp.concatenate(
        [
            jnp.where(left_half(), store[index_ref[k, row]], store[index_ref[k + 1, row]])
            for k in range(first, first + NEAR, 2)
        ],
        axis=1,
    )


def fold_kernel(
    _, raw_hbm, slot_hbm, live_hbm, scale_hbm, time_hbm,
    __, tile_out, edge_out, index_out, mine_out, theirs_out, time_out,
    raw_ref, slot_ref, live_ref, scale_ref, time_ref, arrived, *, rim_count,
):
    count = slot_ref.shape[1]
    rows = raw_ref.shape[0] // PARTS
    fetches = [
        pltpu.make_async_copy(source, target, arrived.at[n])
        for n, (source, target) in enumerate(
            [(scale_hbm, scale_ref), (slot_hbm, slot_ref), (live_hbm, live_ref), (time_hbm, time_ref)]
            + [
                (raw_hbm.at[pl.ds(p * rows, rows)], raw_ref.at[pl.ds(p * rows, rows)])
                for p in range(PARTS)
            ]
        )
    ]
    for fetch in fetches:
        fetch.start()
    half = lax.broadcasted_iota(jnp.int32, (PB, LANES), 1) < PB
    small = len(fetches) - PARTS
    for fetch in fetches[:small]:
        fetch.wait()
    eye = [lax.broadcasted_iota(jnp.int32, (FEATURES, FEATURES), n) for n in range(2)]
    column = jnp.where(eye[0] == eye[1], time_ref[...], 0.0)
    time_out[...] = jnp.sum(column, axis=1, keepdims=True)
    indices = source_index(slot_ref[...], live_ref[...], count, rim_count)
    for out, index in zip((index_out, mine_out, theirs_out), indices):
        out[...] = index
    for p in range(PARTS):
        fetches[small + p].wait()
        for b in range(p * rows // PB, (p + 1) * rows // PB):
            for k in range(0, scale_ref.shape[0], 2):
                at = pl.ds(b * PB, PB), pl.ds(k * PB, LANES)
                scale = jnp.where(half, scale_ref[k, b], scale_ref[k + 1, b])
                scaled = (raw_ref[at].astype(jnp.float32) * scale).astype(tile_out.dtype)
                tile_out[at] = scaled
                if b < rim_count and k >= NEAR:
                    edge_out[pl.ds(b * PB, PB), pl.ds((k - NEAR) * PB, LANES)] = scaled


def near_kernel(index_ref, value_ref, tile_ref, near_out, store):
    for t in range(value_ref.shape[1] // LANES):
        spread(value_ref[:, t * LANES : (t + 1) * LANES], store, 2 * t)
    clear_last(store)
    for t in range(near_out.shape[1] // LANES):
        at = pl.ds(t * LANES, LANES)
        near_out[:, at] = product(
            picked(store, index_ref, 0, 2 * t),
            picked(store, index_ref, 0, 2 * t + 1),
            tile_ref[at, : NEAR * PB],
        )


def clear_last(store):
    store[store.shape[0] - 1] = jnp.zeros(store.shape[1:], store.dtype)


def part_kernel(
    index_ref, mine_ref, theirs_ref, received_ref, both_ref, tile_ref, value_ref, edge_ref,
    part_out, store,
):
    def keep(pair, number):
        store[number // 2] = pair

    panels, _, rim = received_ref.shape
    each_pair(received_ref, 0, keep)
    each_pair(both_ref.at[pl.ds(0, 1)], panels * (rim // PB), keep)
    clear_last(store)

    def own_pair(number):
        return value_ref[:, pl.ds(pl.multiple_of((number >> 1) * LANES, LANES), LANES)]

    def far_pair(number):
        return store[number >> 1]

    def sources(fetch, blank, index_ref, first, row):
        parts = []
        for k in range(first, first + NEAR, 2):
            halves = []
            for side in range(2):
                number = index_ref[k + side, row]
                if blank is None:
                    pair = fetch(number)
                else:
                    pair = fetch(jnp.minimum(number, blank - 1))
                    pair = jnp.where(number < blank, pair, jnp.zeros_like(pair))
                halves.append(jnp.where((number & 1) == side, pair, turn(pair)))
            parts.append(jnp.where(left_half(), halves[0], halves[1]))
        return jnp.concatenate(parts, axis=1)

    count = value_ref.shape[1] // PB
    for t in range(rim // LANES):
        at = pl.ds(t * LANES, LANES)
        rows = (2 * t, 2 * t + 1)
        near = product(
            *(sources(own_pair, count, index_ref, 0, row) for row in rows), tile_ref[at, : NEAR * PB]
        )
        far = product(
            *(sources(far_pair, None, mine_ref, NEAR, row) for row in rows),
            tile_ref[at, NEAR * PB :],
        )
        part_out[0, :, at] = near + far
        part_out[1, :, at] = product(
            *(sources(far_pair, None, theirs_ref, NEAR, row) for row in rows), edge_ref[at, :]
        )


def far_kernel(step, last, index_ref, *refs):
    if not last:
        refs = refs[1:]
    received_ref, others_ref, both_ref, tile_ref, near_ref, times_ref, total_ref = refs[:7]
    if last:
        result_hbm, store, total_out, sent = refs[7:]
    else:
        _, total_out, value_out, store, *fetching = refs[7:]
        if fetching:
            features_hbm, (total_ref, arrived) = total_ref, fetching
            fetch = pltpu.make_async_copy(features_hbm, total_ref, arrived)
            fetch.start()
    panels, _, rim = received_ref.shape
    rim_count = rim // PB

    def keep(pair, number):
        spread(pair, store, number)

    each_pair(received_ref, 0, keep)
    each_pair(others_ref, panels * rim_count, keep)
    each_pair(both_ref.at[pl.ds(1, 1)], 2 * panels * rim_count, keep)
    each_pair(both_ref.at[pl.ds(0, 1)], (2 * panels + 1) * rim_count, keep)
    clear_last(store)
    if not last and fetching:
        fetch.wait()
    factor = jnp.ones(times_ref.shape, jnp.float32)
    for n in range(1, step + 1):
        factor = factor * -times_ref[...] / jnp.float32(n)
    pairs = near_ref.shape[1] // LANES
    sends = []
    for t in range(pairs):
        at = pl.ds(t * LANES, LANES)
        image = near_ref[:, at] + product(
            picked(store, index_ref, NEAR, 2 * t),
            picked(store, index_ref, NEAR, 2 * t + 1),
            tile_ref[at, NEAR * PB :],
        )
        total = total_ref[:, at].astype(jnp.float32) + factor * image
        total_out[:, at] = total.astype(total_out.dtype)
        if not last:
            value_out[:, at] = image.astype(value_out.dtype)
        elif (t + 1) % (pairs // PARTS) == 0:
            part = pl.ds((t + 1 - pairs // PARTS) * LANES, pairs // PARTS * LANES)
            send = pltpu.make_async_copy(
                total_out.at[:, part], result_hbm.at[:, part], sent.at[len(sends)]
            )
            send.start()
            sends.append(send)
    for send in sends:
        send.wait()


def call(kernel, results, scratch, flops, scalars, *arrays, fetched=(), through=None, to_hbm=False):
    handed = () if through is None else (through,)
    out_shape = tuple(jax.ShapeDtypeStruct(x.shape, x.dtype) for x in handed) + results
    anywhere, vmem = pl.BlockSpec(memory_space=pl.ANY), pl.BlockSpec(memory_space=pltpu.VMEM)
    hbm = pl.BlockSpec(memory_space=pltpu.HBM)
    fetched = [pltpu.with_memory_space_constraint(x, pltpu.HBM) for x in fetched]
    return pl.pallas_call(
        kernel,
        out_shape=out_shape,
        in_specs=[pl.BlockSpec(memory_space=pltpu.SMEM)] * len(scalars)
        + [anywhere] * len(handed)
        + [vmem] * len(arrays)
        + [hbm] * len(fetched),
        out_specs=(anywhere,) * len(handed) + (hbm if to_hbm else vmem,) * len(results),
        scratch_shapes=scratch,
        input_output_aliases={len(scalars): 0} if handed else {},
        compiler_params=pltpu.CompilerParams(vmem_limit_bytes=VMEM_MIB * 1024 * 1024),
        cost_estimate=pl.CostEstimate(flops=flops, bytes_accessed=flops // 64, transcendentals=0),
    )(*scalars, *handed, *arrays, *fetched)


def body(features, tiles, scales, slots, live, times):
    count, width = tiles.shape[2], tiles.shape[4]
    slot_count = scales.shape[3]
    rim_count = max(1, count // 8)
    points = count * PB
    rim_points = rim_count * PB
    value = features.reshape(FEATURES, points)
    rim = value[:, :rim_points]
    both = jnp.stack([rim, swap_cores(rim)])
    scales = scales.reshape(count, slot_count).T
    slots = slots.reshape(count, slot_count).T
    times_row = times.reshape(1, FEATURES)
    chips = len(partners())
    half = FEATURES * points * width

    def blocks(number):
        return pltpu.VMEM((number, FEATURES, LANES), jnp.bfloat16)

    own_store = blocks(count + 1)
    far_store = blocks((2 * chips + 2) * rim_count + 1)
    part_store = blocks((chips + 1) * rim_count // 2 + 1)
    image_shape = jax.ShapeDtypeStruct(value.shape, jnp.float32)
    value_shape = jax.ShapeDtypeStruct(value.shape, jnp.bfloat16)
    part_shape = jax.ShapeDtypeStruct(both.shape, jnp.float32)
    tile_shape = jax.ShapeDtypeStruct((points, width), jnp.bfloat16)
    edge_shape = jax.ShapeDtypeStruct((rim_points, width - NEAR * PB), jnp.bfloat16)
    index_shape = jax.ShapeDtypeStruct(slots.shape, jnp.int32)
    time_shape = jax.ShapeDtypeStruct((FEATURES, 1), jnp.float32)

    def image(value, scaled, index):
        return call(near_kernel, (image_shape,), [own_store], half, (index,), value, scaled)[0]

    def fold(through):
        through, scaled, edge, index, mine, theirs, times = fold_call(through)
        edge, theirs = swap_cores(edge), swap_cores(theirs)
        through, edge, theirs = lax.optimization_barrier((through, edge, theirs))
        return through, scaled, edge, index, mine, theirs, times

    def fold_call(through):
        return call(
            functools.partial(fold_kernel, rim_count=rim_count),
            (tile_shape, edge_shape, index_shape, index_shape, index_shape, time_shape),
            [
                pltpu.VMEM((points, width), jnp.bfloat16),
                pltpu.VMEM(slots.shape, jnp.int32),
                pltpu.VMEM((1, count), jnp.int32),
                pltpu.SMEM(scales.shape, jnp.float32),
                pltpu.VMEM((1, FEATURES), jnp.float32),
                pltpu.SemaphoreType.DMA((PARTS + 4,)),
            ],
            half,
            (),
            fetched=(
                tiles.reshape(points, width),
                slots,
                live.reshape(1, count),
                scales,
                times_row,
            ),
            through=through,
        )

    received, (scaled, edge, index, mine, theirs, times) = exchange(both, fold, True)
    total = value
    for step in range(1, TERMS):
        others = swap_cores(received)
        (part,) = call(
            part_kernel,
            (part_shape,),
            [part_store],
            half // 4,
            (index, mine, theirs),
            *(received, both, scaled, value, edge),
        )

        def rest(through):
            begun = step > 1
            fetch = [pltpu.VMEM(value.shape, jnp.bfloat16), pltpu.SemaphoreType.DMA]
            through, total_now, value_now = call(
                functools.partial(far_kernel, step, False),
                (image_shape, value_shape),
                [far_store] + ([] if begun else fetch),
                half,
                *arrays,
                *([total] if begun else []),
                fetched=() if begun else (features.reshape(total.shape),),
                through=through,
            )
            return through, total_now, value_now

        near = image(value, scaled, index)
        added, others, near = lax.optimization_barrier((swap_cores(part), others, near))
        arrays = ((index,), received, others, both, scaled, near, times)
        both = (part + added[::-1]).astype(jnp.bfloat16)
        received, (total, value) = exchange(both, rest, False)
    near = image(value, scaled, index)
    (out,) = call(
        functools.partial(far_kernel, TERMS, True),
        (value_shape,),
        [
            far_store,
            pltpu.VMEM(value.shape, jnp.bfloat16),
            pltpu.SemaphoreType.DMA((PARTS,)),
        ],
        half,
        (index,),
        received,
        swap_cores(received),
        both,
        scaled,
        near,
        times,
        total,
        to_hbm=True,
    )
    return out.reshape(features.shape)


def solution(mesh):
    return jax.shard_map(
        body,
        mesh=mesh,
        in_specs=(
            P(None, "gx", "gy", "gz"),
            P("gx", "gy", "gz", None, None),
            P("gx", "gy", "gz", None),
            P("gx", "gy", "gz", None),
            P("gx", "gy", "gz"),
            P(),
        ),
        out_specs=P(None, "gx", "gy", "gz"),
        check_vma=False,
    )
```

```python
import functools

import jax
import jax.numpy as jnp
from jax import lax
from jax.experimental import pallas as pl
from jax.experimental.pallas import tpu as pltpu
from jax.sharding import PartitionSpec as P

PB = 64
TERMS = 3
FEATURES = 64
NEAR = 4
PARTS = 8
VMEM_MIB = 16
LANES = 2 * PB
AXES = ("gx", "gy", "gz")


def pairings(count):
    first = [(i, i ^ 1) for i in range(count)]
    second = [(i, (i + 1) % count if i % 2 else (i - 1) % count) for i in range(count)]
    return [first] if count == 2 else [first, second]


def partner_rank(here, step, count):
    forward = jnp.where((here & 1) == 0, 1, 2)
    backward = 3 - forward
    rank = jnp.where(step == 1, 0, jnp.where(step == 2, forward, backward))
    there = here + step - 1
    return rank, (there >= 0) & (there < count)


def place(rank, here, count):
    there = here if rank == 0 else dict(pairings(count)[rank - 1])[here]
    return there if abs(there - here) <= 1 else None


def partners():
    x_count = len(pairings(lax.axis_size("gx"))) + 1
    y_count = len(pairings(lax.axis_size("gy"))) + 1
    pair_count = lax.axis_size("gz") // 2
    chips = [(x, b) for x in range(x_count) for b in range(pair_count)]
    side = [(x, y, b) for x, b in chips for y in range(1, y_count)]
    return side + [(x, 0, b) for x, b in chips[1:]]


def partner_number(x, y, b):
    x_count = len(pairings(lax.axis_size("gx"))) + 1
    y_count = len(pairings(lax.axis_size("gy"))) + 1
    pair_count = lax.axis_size("gz") // 2
    chip = x * pair_count + b
    return jnp.where(
        y > 0, chip * (y_count - 1) + y - 1, x_count * pair_count * (y_count - 1) + chip - 1
    )


def swap(value, by_core):
    sizes = [lax.axis_size(name) for name in AXES]
    pairs = []
    for i in range(sizes[0]):
        for j in range(sizes[1]):
            for k in range(sizes[2]):
                x, y, b = by_core[k % 2]
                to = (place(x, i, sizes[0]), place(y, j, sizes[1]), (k // 2 ^ b) * 2 + k % 2)
                if None in to:
                    to = (i, j, (k // 2 ^ 1) * 2 + k % 2)
                pairs.append(
                    ((i * sizes[1] + j) * sizes[2] + k, (to[0] * sizes[1] + to[1]) * sizes[2] + to[2])
                )
    return lax.ppermute(value, AXES, pairs)


def swap_cores(value):
    return lax.ppermute(value, "gz", [(k, k ^ 1) for k in range(lax.axis_size("gz"))])


def exchange(both, work, far_first):
    chips = partners()
    sides = len(pairings(lax.axis_size("gy")))
    plane = chips[-((len(chips) - sides) // (sides + 1)) :]
    rim = both[0]
    side = swap(both, (chips[0], chips[sides - 1]))
    own = [
        swap(both, (plane[t], plane[t + 1])) for t in range(0, len(plane) - len(plane) % 2, 2)
    ]
    step = -1 if far_first else 1
    passed = [swap(side, (chip, chip)) for chip in plane[::step]]
    alone = [swap(rim, (plane[-1], plane[-1]))] if len(plane) % 2 else []
    passed[0], *results = work(passed[0])
    received = jnp.concatenate([side] + passed[::step] + own + [panel[None] for panel in alone])
    return received, results


def source_index(slots, live, count, rim_count):
    layers = lax.axis_size("gz")
    x_at, y_at, z_at = (lax.axis_index(name) for name in AXES)
    rest = jnp.maximum(slots - count, 0)
    column = sum((rest >= rim_count * layers * n).astype(jnp.int32) for n in range(1, 9))
    a = (column >= 3).astype(jnp.int32) + (column >= 6).astype(jnp.int32)
    c = column - 3 * a
    inside = rest - rim_count * layers * column
    m = sum((inside >= rim_count * n).astype(jnp.int32) for n in range(1, layers))
    r = inside - rim_count * m
    x_rank, x_in = partner_rank(x_at, a, lax.axis_size("gx"))
    y_rank, y_in = partner_rank(y_at, c, lax.axis_size("gy"))
    flip = (m >> 1) ^ (z_at >> 1)
    chips = len(partners())
    core, target = z_at & 1, m & 1
    number = partner_number(x_rank, y_rank, flip)
    holder, panel = number & 1, (number & -2) + (target ^ (number & 1))
    if chips % 2:
        holder = jnp.where(number == chips - 1, target, holder)
        panel = jnp.where(number == chips - 1, chips - 1, panel)
    here = (x_rank == 0) & (y_rank == 0) & (flip == 0)
    place = lax.broadcasted_iota(jnp.int32, slots.shape, 0)
    used = place < live
    there = x_in & y_in & used
    all_rims = jnp.where(
        here,
        2 * chips + jnp.where(target == core, 1, 0),
        panel + jnp.where(holder == core, 0, chips),
    )
    far = jnp.where(there, all_rims * rim_count + r, (2 * chips + 2) * rim_count)
    index = jnp.where(place < NEAR, jnp.where(used, slots, count), far)
    held = jnp.where(here, chips, panel) * rim_count + r
    holder = jnp.where(here, target, holder)
    zero = (chips + 1) * rim_count
    return index, *(jnp.where(there & (holder == at), held, zero) for at in (core, 1 - core))


def left_half():
    return lax.broadcasted_iota(jnp.int32, (FEATURES, LANES), 1) < PB


def turn(pair):
    return jnp.concatenate([pair[:, PB:], pair[:, :PB]], axis=1)


def spread(pair, store, at):
    turned = turn(pair)
    store[at] = jnp.where(left_half(), pair, turned)
    store[at + 1] = jnp.where(left_half(), turned, pair)


def each_pair(panels_ref, first, place_pair):
    rim = panels_ref.shape[2]
    for panel in range(panels_ref.shape[0]):
        for t in range(rim // LANES):
            place_pair(
                panels_ref[panel, :, t * LANES : (t + 1) * LANES],
                first + panel * (rim // PB) + 2 * t,
            )


def product(first, second, tile):
    both = lax.dot_general(
        jnp.concatenate([first, second], axis=0),
        tile,
        (((1,), (1,)), ((), ())),
        preferred_element_type=jnp.float32,
    )
    return jnp.where(left_half(), both[:FEATURES], both[FEATURES:])


def picked(store, index_ref, first, row):
    return jnp.concatenate(
        [
            jnp.where(left_half(), store[index_ref[k, row]], store[index_ref[k + 1, row]])
            for k in range(first, first + NEAR, 2)
        ],
        axis=1,
    )


def fold_kernel(
    _, raw_hbm, slot_hbm, live_hbm, scale_hbm, time_hbm,
    __, tile_out, edge_out, index_out, mine_out, theirs_out, time_out,
    raw_ref, slot_ref, live_ref, scale_ref, time_ref, arrived, *, rim_count,
):
    count = slot_ref.shape[1]
    rows = raw_ref.shape[0] // PARTS
    fetches = [
        pltpu.make_async_copy(source, target, arrived.at[n])
        for n, (source, target) in enumerate(
            [(scale_hbm, scale_ref), (slot_hbm, slot_ref), (live_hbm, live_ref), (time_hbm, time_ref)]
            + [
                (raw_hbm.at[pl.ds(p * rows, rows)], raw_ref.at[pl.ds(p * rows, rows)])
                for p in range(PARTS)
            ]
        )
    ]
    for fetch in fetches:
        fetch.start()
    half = lax.broadcasted_iota(jnp.int32, (PB, LANES), 1) < PB
    small = len(fetches) - PARTS
    for fetch in fetches[:small]:
        fetch.wait()
    eye = [lax.broadcasted_iota(jnp.int32, (FEATURES, FEATURES), n) for n in range(2)]
    column = jnp.where(eye[0] == eye[1], time_ref[...], 0.0)
    time_out[...] = jnp.sum(column, axis=1, keepdims=True)
    indices = source_index(slot_ref[...], live_ref[...], count, rim_count)
    for out, index in zip((index_out, mine_out, theirs_out), indices):
        out[...] = index
    for p in range(PARTS):
        fetches[small + p].wait()
        for b in range(p * rows // PB, (p + 1) * rows // PB):
            for k in range(0, scale_ref.shape[0], 2):
                at = pl.ds(b * PB, PB), pl.ds(k * PB, LANES)
                scale = jnp.where(half, scale_ref[k, b], scale_ref[k + 1, b])
                scaled = (raw_ref[at].astype(jnp.float32) * scale).astype(tile_out.dtype)
                tile_out[at] = scaled
                if b < rim_count and k >= NEAR:
                    edge_out[pl.ds(b * PB, PB), pl.ds((k - NEAR) * PB, LANES)] = scaled


def near_kernel(index_ref, value_ref, tile_ref, near_out, store):
    for t in range(value_ref.shape[1] // LANES):
        spread(value_ref[:, t * LANES : (t + 1) * LANES], store, 2 * t)
    clear_last(store)
    for t in range(near_out.shape[1] // LANES):
        at = pl.ds(t * LANES, LANES)
        near_out[:, at] = product(
            picked(store, index_ref, 0, 2 * t),
            picked(store, index_ref, 0, 2 * t + 1),
            tile_ref[at, : NEAR * PB],
        )


def clear_last(store):
    store[store.shape[0] - 1] = jnp.zeros(store.shape[1:], store.dtype)


def part_kernel(
    index_ref, mine_ref, theirs_ref, received_ref, both_ref, tile_ref, value_ref, edge_ref,
    part_out, store,
):
    def keep(pair, number):
        store[number // 2] = pair

    panels, _, rim = received_ref.shape
    each_pair(received_ref, 0, keep)
    each_pair(both_ref.at[pl.ds(0, 1)], panels * (rim // PB), keep)
    clear_last(store)

    def own_pair(number):
        return value_ref[:, pl.ds(pl.multiple_of((number >> 1) * LANES, LANES), LANES)]

    def far_pair(number):
        return store[number >> 1]

    def sources(fetch, blank, index_ref, first, row):
        parts = []
        for k in range(first, first + NEAR, 2):
            halves = []
            for side in range(2):
                number = index_ref[k + side, row]
                if blank is None:
                    pair = fetch(number)
                else:
                    pair = fetch(jnp.minimum(number, blank - 1))
                    pair = jnp.where(number < blank, pair, jnp.zeros_like(pair))
                halves.append(jnp.where((number & 1) == side, pair, turn(pair)))
            parts.append(jnp.where(left_half(), halves[0], halves[1]))
        return jnp.concatenate(parts, axis=1)

    count = value_ref.shape[1] // PB
    for t in range(rim // LANES):
        at = pl.ds(t * LANES, LANES)
        rows = (2 * t, 2 * t + 1)
        near = product(
            *(sources(own_pair, count, index_ref, 0, row) for row in rows), tile_ref[at, : NEAR * PB]
        )
        far = product(
            *(sources(far_pair, None, mine_ref, NEAR, row) for row in rows),
            tile_ref[at, NEAR * PB :],
        )
        part_out[0, :, at] = near + far
        part_out[1, :, at] = product(
            *(sources(far_pair, None, theirs_ref, NEAR, row) for row in rows), edge_ref[at, :]
        )


def far_kernel(step, last, index_ref, *refs):
    if not last:
        refs = refs[1:]
    received_ref, others_ref, both_ref, tile_ref, near_ref, times_ref, total_ref = refs[:7]
    if last:
        result_hbm, store, total_out, sent = refs[7:]
    else:
        _, total_out, value_out, store, *fetching = refs[7:]
        if fetching:
            features_hbm, (total_ref, arrived) = total_ref, fetching
            fetch = pltpu.make_async_copy(features_hbm, total_ref, arrived)
            fetch.start()
    panels, _, rim = received_ref.shape
    rim_count = rim // PB

    def keep(pair, number):
        spread(pair, store, number)

    each_pair(received_ref, 0, keep)
    each_pair(others_ref, panels * rim_count, keep)
    each_pair(both_ref.at[pl.ds(1, 1)], 2 * panels * rim_count, keep)
    each_pair(both_ref.at[pl.ds(0, 1)], (2 * panels + 1) * rim_count, keep)
    clear_last(store)
    if not last and fetching:
        fetch.wait()
    factor = jnp.ones(times_ref.shape, jnp.float32)
    for n in range(1, step + 1):
        factor = factor * -times_ref[...] / jnp.float32(n)
    pairs = near_ref.shape[1] // LANES
    sends = []
    for t in range(pairs):
        at = pl.ds(t * LANES, LANES)
        image = near_ref[:, at] + product(
            picked(store, index_ref, NEAR, 2 * t),
            picked(store, index_ref, NEAR, 2 * t + 1),
            tile_ref[at, NEAR * PB :],
        )
        total = total_ref[:, at].astype(jnp.float32) + factor * image
        total_out[:, at] = total.astype(total_out.dtype)
        if not last:
            value_out[:, at] = image.astype(value_out.dtype)
        elif (t + 1) % (pairs // PARTS) == 0:
            part = pl.ds((t + 1 - pairs // PARTS) * LANES, pairs // PARTS * LANES)
            send = pltpu.make_async_copy(
                total_out.at[:, part], result_hbm.at[:, part], sent.at[len(sends)]
            )
            send.start()
            sends.append(send)
    for send in sends:
        send.wait()


def call(kernel, results, scratch, flops, scalars, *arrays, fetched=(), through=None, to_hbm=False):
    handed = () if through is None else (through,)
    out_shape = tuple(jax.ShapeDtypeStruct(x.shape, x.dtype) for x in handed) + results
    anywhere, vmem = pl.BlockSpec(memory_space=pl.ANY), pl.BlockSpec(memory_space=pltpu.VMEM)
    hbm = pl.BlockSpec(memory_space=pltpu.HBM)
    fetched = [pltpu.with_memory_space_constraint(x, pltpu.HBM) for x in fetched]
    return pl.pallas_call(
        kernel,
        out_shape=out_shape,
        in_specs=[pl.BlockSpec(memory_space=pltpu.SMEM)] * len(scalars)
        + [anywhere] * len(handed)
        + [vmem] * len(arrays)
        + [hbm] * len(fetched),
        out_specs=(anywhere,) * len(handed) + (hbm if to_hbm else vmem,) * len(results),
        scratch_shapes=scratch,
        input_output_aliases={len(scalars): 0} if handed else {},
        compiler_params=pltpu.CompilerParams(vmem_limit_bytes=VMEM_MIB * 1024 * 1024),
        cost_estimate=pl.CostEstimate(flops=flops, bytes_accessed=flops // 64, transcendentals=0),
    )(*scalars, *handed, *arrays, *fetched)


def body(features, tiles, scales, slots, live, times):
    count, width = tiles.shape[2], tiles.shape[4]
    slot_count = scales.shape[3]
    rim_count = max(1, count // 8)
    points = count * PB
    rim_points = rim_count * PB
    value = features.reshape(FEATURES, points)
    rim = value[:, :rim_points]
    both = jnp.stack([rim, swap_cores(rim)])
    scales = scales.reshape(count, slot_count).T
    slots = slots.reshape(count, slot_count).T
    times_row = times.reshape(1, FEATURES)
    chips = len(partners())
    half = FEATURES * points * width

    def blocks(number):
        return pltpu.VMEM((number, FEATURES, LANES), jnp.bfloat16)

    own_store = blocks(count + 1)
    far_store = blocks((2 * chips + 2) * rim_count + 1)
    part_store = blocks((chips + 1) * rim_count // 2 + 1)
    image_shape = jax.ShapeDtypeStruct(value.shape, jnp.float32)
    value_shape = jax.ShapeDtypeStruct(value.shape, jnp.bfloat16)
    part_shape = jax.ShapeDtypeStruct(both.shape, jnp.float32)
    tile_shape = jax.ShapeDtypeStruct((points, width), jnp.bfloat16)
    edge_shape = jax.ShapeDtypeStruct((rim_points, width - NEAR * PB), jnp.bfloat16)
    index_shape = jax.ShapeDtypeStruct(slots.shape, jnp.int32)
    time_shape = jax.ShapeDtypeStruct((FEATURES, 1), jnp.float32)

    def image(value, scaled, index):
        return call(near_kernel, (image_shape,), [own_store], half, (index,), value, scaled)[0]

    def fold(through):
        through, scaled, edge, index, mine, theirs, times = fold_call(through)
        edge, theirs = swap_cores(edge), swap_cores(theirs)
        through, edge, theirs = lax.optimization_barrier((through, edge, theirs))
        return through, scaled, edge, index, mine, theirs, times

    def fold_call(through):
        return call(
            functools.partial(fold_kernel, rim_count=rim_count),
            (tile_shape, edge_shape, index_shape, index_shape, index_shape, time_shape),
            [
                pltpu.VMEM((points, width), jnp.bfloat16),
                pltpu.VMEM(slots.shape, jnp.int32),
                pltpu.VMEM((1, count), jnp.int32),
                pltpu.SMEM(scales.shape, jnp.float32),
                pltpu.VMEM((1, FEATURES), jnp.float32),
                pltpu.SemaphoreType.DMA((PARTS + 4,)),
            ],
            half,
            (),
            fetched=(
                tiles.reshape(points, width),
                slots,
                live.reshape(1, count),
                scales,
                times_row,
            ),
            through=through,
        )

    received, (scaled, edge, index, mine, theirs, times) = exchange(both, fold, True)
    total = value
    for step in range(1, TERMS):
        others = swap_cores(received)
        (part,) = call(
            part_kernel,
            (part_shape,),
            [part_store],
            half // 4,
            (index, mine, theirs),
            *(received, both, scaled, value, edge),
        )

        def rest(through):
            begun = step > 1
            fetch = [pltpu.VMEM(value.shape, jnp.bfloat16), pltpu.SemaphoreType.DMA]
            through, total_now, value_now = call(
                functools.partial(far_kernel, step, False),
                (image_shape, value_shape),
                [far_store] + ([] if begun else fetch),
                half,
                *arrays,
                *([total] if begun else []),
                fetched=() if begun else (features.reshape(total.shape),),
                through=through,
            )
            return through, total_now, value_now

        near = image(value, scaled, index)
        added, others = lax.optimization_barrier((swap_cores(part), others))
        arrays = ((index,), received, others, both, scaled, near, times)
        both = (part + added[::-1]).astype(jnp.bfloat16)
        received, (total, value) = exchange(both, rest, False)
    near = image(value, scaled, index)
    (out,) = call(
        functools.partial(far_kernel, TERMS, True),
        (value_shape,),
        [
            far_store,
            pltpu.VMEM(value.shape, jnp.bfloat16),
            pltpu.SemaphoreType.DMA((PARTS,)),
        ],
        half,
        (index,),
        received,
        swap_cores(received),
        both,
        scaled,
        near,
        times,
        total,
        to_hbm=True,
    )
    return out.reshape(features.shape)


def solution(mesh):
    return jax.shard_map(
        body,
        mesh=mesh,
        in_specs=(
            P(None, "gx", "gy", "gz"),
            P("gx", "gy", "gz", None, None),
            P("gx", "gy", "gz", None),
            P("gx", "gy", "gz", None),
            P("gx", "gy", "gz"),
            P(),
        ),
        out_specs=P(None, "gx", "gy", "gz"),
        check_vma=False,
    )
```
